32 devices in a mesh: tile: 4 (over y, x), orient: 8 (over z, core).
Axes of the slice: x: 2, y: 2, z: 4, core: 2. Of those that a mesh axis runs over, the one named last changes fastest.
Arguments:
- micrograph_tiles: bfloat16 [8, 512, 512], P('tile'), as said below
- tile_offsets: int32 [8, 2], P('tile'), may hold values from 0 to 3584
- library: bfloat16 [32, 8, 128, 128], P('tile', 'orient'), as said below
- orient_ids: int32 [8, 2], P('orient'), may hold values from 0 to 31
Outputs:
- peak_score: float32 [8, 384, 384], P('tile')
- z_score: float32 [8, 384, 384], P('tile')
The draws below stay inside these ranges and needn't reach their ends.
Inputs may be any that keep to these rules, and one draw needn't show every extreme that they name: `micrograph_tiles`: real-valued pixel intensities of the tiles. `library`: real-valued projection densities.
All inputs are finite; a program needn't handle non-finite values.
Results may differ from the reference program's by a relative error of at most 0.0095.
Values may be sent and summed in bfloat16 or wider, within the bound.
A program may use at most 64 MiB of HBM per device.

```python
import math
import jax
import jax.numpy as jnp
from jax import lax

PAD = 512
TPL = 128
VALID = 384
STEPS = 2
TILES = 8
LIB = 32
SHARDS = 8
SEARCH = 16


def draw_micrograph_tiles(key, part):
    subkeys = jax.random.split(key, 4)
    base_draw = jax.random.truncated_normal(subkeys[0], -6.0, 6.0, (TILES, PAD, PAD), jnp.float32)
    ramp_values = jnp.arange(TILES, dtype=jnp.float32) / max(TILES - 1, 1)
    tile_scale = jnp.exp(math.log(3.0) * ramp_values + jax.random.uniform(subkeys[1], (TILES,), jnp.float32, 0.0, math.log(4.0)))
    row_scale = jnp.exp(jax.random.uniform(subkeys[2], (TILES, PAD, 1), jnp.float32, 0.0, math.log(10.0)))
    col_scale = jnp.exp(jax.random.uniform(subkeys[3], (TILES, 1, PAD), jnp.float32, 0.0, math.log(10.0)))
    return (base_draw * tile_scale[:, None, None] * row_scale * col_scale).astype(jnp.bfloat16)


def draw_library(key, part):
    subkeys = jax.random.split(key, 3)
    base_draw = jax.random.truncated_normal(subkeys[0], -6.0, 6.0, (LIB, SHARDS, TPL, TPL), jnp.float32)
    row_scale = jnp.exp(jax.random.uniform(subkeys[1], (LIB, SHARDS, TPL, 1), jnp.float32, 0.0, math.log(10.0)))
    col_scale = jnp.exp(jax.random.uniform(subkeys[2], (LIB, SHARDS, 1, TPL), jnp.float32, 0.0, math.log(10.0)))
    return (base_draw * row_scale * col_scale).astype(jnp.bfloat16)


def with_ends(drawn, key, smallest, top_value):
    extent = drawn.shape
    place = [jax.random.randint(jax.random.fold_in(key, axis), (), 0, extent[axis]) for axis in range(len(extent))]
    drawn = drawn.at[tuple(place)].set(smallest)
    longest = extent.index(max(extent))
    place[longest] = (place[longest] + 1) % extent[longest]
    return drawn.at[tuple(place)].set(top_value)


def setup_inputs(seed: int = 0) -> dict:
    seeds = jax.random.split(jax.random.key(seed), 5)
    micrograph_tiles = draw_micrograph_tiles(jax.random.fold_in(seeds[4], 71), 0)
    tile_offsets = with_ends(jax.random.randint(seeds[1], (TILES, 2), 0, 3585), jax.random.fold_in(seeds[1], 1), 0, 3584).astype(jnp.int32)
    library = draw_library(jax.random.fold_in(seeds[4], 71), 0)
    orient_ids = with_ends(jax.random.randint(seeds[3], (SHARDS, STEPS), 0, LIB), jax.random.fold_in(seeds[3], 1), 0, LIB - 1).astype(jnp.int32)
    return {"micrograph_tiles": micrograph_tiles, "tile_offsets": tile_offsets, "library": library, "orient_ids": orient_ids}


AMPLITUDE = 0.07
DEFOCUS_BASE = 100.0
DEFOCUS_TILT = 0.002
FLOOR_SHARE = 0.25

def dft_tables(length):
    counter = jnp.arange(length, dtype=jnp.int32)
    product = counter[:, None] * counter[None, :] % length
    angle_table = product.astype(jnp.float32) * (2.0 * math.pi / length)
    return (jnp.cos(angle_table).astype(jnp.bfloat16), jnp.sin(angle_table).astype(jnp.bfloat16))

def frequency_squares(length):
    counter = jnp.arange(length, dtype=jnp.int32)
    signed = jnp.where(counter < length // 2, counter, counter - length)
    frequency = signed.astype(jnp.float32) / length
    return frequency[:, None] * frequency[:, None] + frequency[None, :] * frequency[None, :]

def batched(spec, left_op, right_op):
    return jnp.einsum(spec, left_op.astype(jnp.float32), right_op.astype(jnp.float32))

def forward_tiles(images, cosine_table, sine_table):
    half_real = batched('tij,jk->tik', images, cosine_table).astype(jnp.bfloat16)
    half_imag = (-batched('tij,jk->tik', images, sine_table)).astype(jnp.bfloat16)
    spec_real = batched('ij,tjk->tik', cosine_table, half_real) + batched('ij,tjk->tik', sine_table, half_imag)
    spec_imag = batched('ij,tjk->tik', cosine_table, half_imag) - batched('ij,tjk->tik', sine_table, half_real)
    return (spec_real, spec_imag)

def tile_filters(tile_offsets, whiten, length):
    squares_freq = frequency_squares(length)
    offsets = tile_offsets.astype(jnp.float32)
    defocus = DEFOCUS_BASE + DEFOCUS_TILT * (offsets[:, 0] - offsets[:, 1])
    phase_angle = math.pi * defocus[:, None, None] * squares_freq[None]
    contrast = -(math.sqrt(1.0 - AMPLITUDE * AMPLITUDE) * jnp.sin(phase_angle) + AMPLITUDE * jnp.cos(phase_angle))
    center = jnp.where(squares_freq > 0.0, 1.0, 0.0).astype(jnp.float32)
    return contrast * (whiten * center)[None]

def template_spectrum(template, cosine_table, sine_table):
    pattern_size = template.shape[0]
    tpl_real = jnp.dot(template, cosine_table[:pattern_size], preferred_element_type=jnp.float32).astype(jnp.bfloat16)
    tpl_imag = (-jnp.dot(template, sine_table[:pattern_size], preferred_element_type=jnp.float32)).astype(jnp.bfloat16)
    col_cos = cosine_table[:, :pattern_size]
    col_sin = sine_table[:, :pattern_size]
    base_real = jnp.dot(col_cos, tpl_real, preferred_element_type=jnp.float32) + jnp.dot(col_sin, tpl_imag, preferred_element_type=jnp.float32)
    base_imag = jnp.dot(col_cos, tpl_imag, preferred_element_type=jnp.float32) - jnp.dot(col_sin, tpl_real, preferred_element_type=jnp.float32)
    return (base_real, base_imag)

def correlate(base_real, base_imag, filters, white_real, white_imag, cosine_table, sine_table, valid_rows):
    length = cosine_table.shape[0]
    filt_real = base_real[None] * filters
    filt_imag = base_imag[None] * filters
    energy = lax.optimization_barrier(jnp.mean(filt_real * filt_real + filt_imag * filt_imag, axis=(1, 2), keepdims=True))
    norm_scale = lax.rsqrt(energy + 1e-06)
    norm_real = (filt_real * norm_scale).astype(jnp.bfloat16).astype(jnp.float32)
    norm_imag = (filt_imag * norm_scale).astype(jnp.bfloat16).astype(jnp.float32)
    wide_real = white_real.astype(jnp.float32)
    wide_imag = white_imag.astype(jnp.float32)
    prod_real = (wide_real * norm_real + wide_imag * norm_imag).astype(jnp.bfloat16)
    prod_imag = (wide_imag * norm_real - wide_real * norm_imag).astype(jnp.bfloat16)
    row_cos = cosine_table[:valid_rows]
    row_sin = sine_table[:valid_rows]
    mid_real = (batched('ij,tjk->tik', row_cos, prod_real) - batched('ij,tjk->tik', row_sin, prod_imag)).astype(jnp.bfloat16)
    mid_imag = (batched('ij,tjk->tik', row_cos, prod_imag) + batched('ij,tjk->tik', row_sin, prod_real)).astype(jnp.bfloat16)
    result = batched('tij,jk->tik', mid_real, cosine_table[:, :valid_rows]) - batched('tij,jk->tik', mid_imag, sine_table[:, :valid_rows])
    return result / length

def reference(micrograph_tiles, tile_offsets, library, orient_ids):
    cosine_table, sine_table = dft_tables(PAD)
    spec_real, spec_imag = forward_tiles(micrograph_tiles, cosine_table, sine_table)
    mean_power = lax.optimization_barrier(jnp.sum(spec_real * spec_real + spec_imag * spec_imag, axis=0)) / TILES
    whiten = lax.rsqrt(jnp.maximum(mean_power, FLOOR_SHARE * jnp.mean(mean_power)))
    white_real = (spec_real * whiten[None]).astype(jnp.bfloat16)
    white_imag = (spec_imag * whiten[None]).astype(jnp.bfloat16)
    filters = tile_filters(tile_offsets, whiten, PAD)
    shard_index = jnp.arange(SHARDS, dtype=jnp.int32)
    templates = library[orient_ids, shard_index[:, None]].reshape(SEARCH, TPL, TPL)

    def visit_template(state_tuple, template):
        running_peak, running_sum, squares = state_tuple
        base_real, base_imag = template_spectrum(template, cosine_table, sine_table)
        scores = correlate(base_real, base_imag, filters, white_real, white_imag, cosine_table, sine_table, VALID)
        return ((jnp.maximum(running_peak, scores), running_sum + scores, squares + scores * scores), None)
    initial = (jnp.full((TILES, VALID, VALID), -jnp.inf, jnp.float32), jnp.zeros((TILES, VALID, VALID), jnp.float32), jnp.zeros((TILES, VALID, VALID), jnp.float32))
    (running_peak, running_sum, squares), _ = lax.scan(visit_template, initial, templates)
    mean_score = running_sum / SEARCH
    variance = squares / SEARCH - mean_score * mean_score
    z_score = (running_peak - mean_score) * lax.rsqrt(variance + 1e-06)
    return (running_peak, z_score)
```

```python
import functools
import math

import jax
import jax.numpy as jnp
import numpy as np
from jax import lax
from jax.experimental import pallas as pl
from jax.experimental.pallas import tpu as pltpu
from jax.sharding import PartitionSpec as P

VALID = 384
AMPLITUDE = 0.07
DEFOCUS_BASE = 100.0
DEFOCUS_TILT = 0.002
FLOOR_SHARE = 0.25
f32, bf16 = jnp.float32, jnp.bfloat16
MESH = pl.DeviceIdType.MESH
VMEM = pl.BlockSpec(memory_space=pltpu.VMEM)
SMEM = pl.BlockSpec(memory_space=pltpu.SMEM)
ANY = pl.BlockSpec(memory_space=pl.ANY)
GRANT = 46 * 1024 * 1024


def tables(length, size, valid):
    half, quarter = length // 2, length // 4
    rows = -(-(half + 1) // 16) * 16
    b_index = np.concatenate([np.arange(0, half, 2), np.arange(1, half, 2), [half]])
    a_index = np.concatenate([np.arange(r, length, 4) for r in range(4)])
    j_index = np.arange(length)

    def wave(function, left, right):
        return function((left[:, None] * right[None, :]) % length * (2.0 * np.pi / length))

    first = np.zeros((2, rows, length))
    first[0, : half + 1] = wave(np.cos, b_index, j_index)
    first[1, : half + 1] = -wave(np.sin, b_index, j_index)
    cosine = wave(np.cos, j_index, a_index)
    sine = wave(np.sin, j_index, a_index)
    base, back = [], []
    for r in range(4):
        columns = slice(r * quarter, (r + 1) * quarter)
        c, s = cosine[:size, columns], sine[:size, columns]
        base.append((np.concatenate([c, s]), np.concatenate([-s, c])))
        c = wave(np.cos, a_index[columns], j_index[:quarter])
        s = wave(np.sin, a_index[columns], j_index[:quarter])
        back.append(np.block([[c, s], [-s, c]]))
    last = []
    for parity in range(2):
        b_part = b_index[parity * quarter : (parity + 1) * quarter]
        count = np.where(b_part == 0, 1.0, 2.0)
        c = wave(np.cos, j_index[:half], b_part) * count / length
        s = -wave(np.sin, j_index[:half], b_part) * count / length
        if parity == 0:
            s[:, 0] = np.cos(np.pi * j_index[:half]) / length
        last.append(np.concatenate([c, s], axis=1))

    def narrow(value):
        return np.asarray(value, np.float32).astype(jnp.bfloat16)

    first = first.reshape(2 * rows, length)
    return dict(
        first=narrow(first),
        small=narrow(np.ascontiguousarray(first[:, :size])),
        cos=narrow(cosine),
        sin=narrow(sine),
        base=narrow(np.concatenate([base[2 * p + q][w] for p in range(2) for w in range(2) for q in range(2)], axis=1)),
        back=narrow(np.stack(back)),
        last=narrow(np.stack(last)),
    )


def dot(left, right):
    return jnp.dot(left, right, preferred_element_type=jnp.float32)


def sine_of_turns(turns):
    part = turns - jnp.floor(turns + 0.5)
    mirrored = jnp.where(part > 0.0, 0.5, -0.5) - part
    part = jnp.where(jnp.abs(part) > 0.25, mirrored, part)
    angle = part * (2.0 * math.pi)
    square = angle * angle
    poly = -1.0 / 39916800.0
    for term in (1.0 / 362880.0, -1.0 / 5040.0, 1.0 / 120.0, -1.0 / 6.0, 1.0):
        poly = poly * square + term
    return angle * poly


def row_index(rows, half):
    row = lax.broadcasted_iota(jnp.int32, (rows, 1), 0)
    quarter = half // 2
    return row, jnp.where(row < quarter, 2 * row, jnp.where(row < half, 2 * row - half + 1, row))


def row_weight(rows, half):
    row, b_index = row_index(rows, half)
    single = (b_index == 0) | (row == half)
    return jnp.where(row > half, 0.0, jnp.where(single, 1.0, 2.0)).astype(f32)


def tile_contrast(tilt, con_ref):
    rows, length = con_ref.shape
    half, quarter = length // 2, length // 4
    row, b_index = row_index(rows, half)
    b_index = jnp.where(row > half, 0, b_index).astype(f32) / length
    lane = lax.broadcasted_iota(jnp.int32, (1, length), 1)
    a_index = 4 * lax.rem(lane, quarter) + lane // quarter
    a_index = jnp.where(a_index < half, a_index, a_index - length).astype(f32) / length
    s2 = a_index * a_index + b_index * b_index
    defocus = DEFOCUS_BASE + DEFOCUS_TILT * tilt
    shift = math.asin(AMPLITUDE) / (2.0 * math.pi)
    contrast = -sine_of_turns(s2 * (0.5 * defocus) + shift)
    con_ref[...] = jnp.where(s2 > 0.0, contrast, 0.0)


def template_spectra(images, small_ref, table_ref, base_ref, power_ref, place):
    rows = small_ref.shape[0] // 2
    size = images.shape[0]
    half = table_ref.shape[1] // 4
    halves = dot(small_ref[...], images).astype(bf16)
    for n in range(images.shape[1] // size):
        columns = slice(n * size, (n + 1) * size)
        joined = jnp.concatenate([halves[:rows, columns], halves[rows:, columns]], axis=1)
        for side in range(2):
            at = 2 * side * half
            real = dot(joined, table_ref[:, at : at + half])
            imag = dot(joined, table_ref[:, at + half : at + 2 * half])
            base_ref[place(n), :, at : at + half] = real.astype(bf16)
            base_ref[place(n), :, at + half : at + 2 * half] = imag.astype(bf16)
            power_ref[place(n), :, side * half : (side + 1) * half] = (real * real + imag * imag).astype(bf16)


def tile_gains(tiles, total_ref, real_ref, imag_ref, con_ref, g_real, g_imag, g_energy):
    rows, length = real_ref.shape
    half = length // 2
    weight = row_weight(rows, half)
    mean = (jnp.sum(total_ref[0] * weight) + jnp.sum(total_ref[1] * weight)) / tiles
    floor = FLOOR_SHARE * (mean / (length * length))
    for side in range(2):
        columns = slice(side * half, (side + 1) * half)
        whiten2 = 1.0 / jnp.maximum(total_ref[side] / tiles, floor)
        contrast = con_ref[:, columns]
        gain = contrast * whiten2
        g_real[:, columns] = (real_ref[:, columns] * gain).astype(bf16)
        g_imag[:, columns] = (imag_ref[:, columns] * gain).astype(bf16)
        g_energy[:, columns] = (contrast * gain * (weight / (length * length))).astype(bf16)


def energy(t, power_ref, g_energy, part_ref):
    rows, length = g_energy.shape
    share = power_ref[t] * g_energy[...]
    share = share[:, : length // 2] + share[:, length // 2 :]
    total = None
    for row in range(0, rows, 16):
        piece = share[row : row + 8] + share[row + 8 : row + 16]
        piece = piece.astype(f32)
        total = piece if total is None else total + piece
    part_ref[t] = total[:, : length // 4] + total[:, length // 4 :]


def half_back(t, column, base_ref, back_ref, g_real, g_imag, mids):
    rows, length = g_real.shape
    quarter = length // 4
    half = 2 * quarter
    found = []
    for side in range(2):
        columns = slice(side * half, (side + 1) * half)
        at = 2 * side * half
        base_real = base_ref[t, :, at : at + half]
        base_imag = base_ref[t, :, at + half : at + 2 * half]
        gain_real, gain_imag = g_real[:, columns], g_imag[:, columns]
        prod_real = gain_real * base_real + gain_imag * base_imag
        prod_imag = gain_imag * base_real - gain_real * base_imag
        for q in range(2):
            part = slice(q * quarter, (q + 1) * quarter)
            joined = jnp.concatenate([prod_real[:, part], prod_imag[:, part]], axis=1)
            found.append(dot(joined, back_ref[2 * side + q]))
    plus02, minus02 = found[0] + found[2], found[0] - found[2]
    plus13, minus13 = found[1] + found[3], found[1] - found[3]
    real, imag = slice(0, quarter), slice(quarter, 2 * quarter)
    out = (
        (plus02[:, real] + plus13[:, real], plus02[:, imag] + plus13[:, imag]),
        (minus02[:, real] - minus13[:, imag], minus02[:, imag] + minus13[:, real]),
        (plus02[:, real] - plus13[:, real], plus02[:, imag] - plus13[:, imag]),
    )
    row = lax.broadcasted_iota(jnp.int32, (quarter, quarter), 0)
    for k, (mid_real, mid_imag) in enumerate(out):
        top = jnp.where(row == 0, mid_real[2 * quarter : 2 * quarter + 1], mid_imag[:quarter])
        mids[k, 0:quarter, column] = mid_real[:quarter].astype(bf16)
        mids[k, quarter : 2 * quarter, column] = top.astype(bf16)
        mids[k, 2 * quarter : 3 * quarter, column] = mid_real[quarter : 2 * quarter].astype(bf16)
        mids[k, 3 * quarter : 4 * quarter, column] = mid_imag[quarter : 2 * quarter].astype(bf16)


def scales_of(part_ref, count):
    return [lax.rsqrt(jnp.sum(part_ref[t]) + 1e-06) for t in range(count)]


def statistics(k, n, fresh, scales, mids, last_ref, stat_ref):
    quarter = last_ref.shape[1] // 2
    half = 2 * quarter
    columns = slice(n * half, (n + 1) * half)
    even = dot(last_ref[0], mids[k, :half, columns])
    odd = dot(last_ref[1], mids[k, half:, columns])
    one, two = scales
    for rows, (e, o) in ((slice(0, half), (even, odd)), (slice(half, half + quarter), (even[:quarter], -odd[:quarter]))):
        left = (e[:, :quarter] + o[:, :quarter]) * one
        right = (e[:, quarter:] + o[:, quarter:]) * two
        top, add, square = jnp.maximum(left, right), left + right, left * left + right * right
        if not fresh:
            top = jnp.maximum(stat_ref[0, rows], top)
            add = stat_ref[1, rows] + add
            square = stat_ref[2, rows] + square
        stat_ref[0, rows] = top
        stat_ref[1, rows] = add
        stat_ref[2, rows] = square


def finish(stats, searched):
    peak, add, squares = stats
    mean = add / searched
    variance = squares / searched - mean * mean
    return peak, (peak - mean) * lax.rsqrt(variance + 1e-06)


def search_kernel(
    n_tile, n_orient, valid,
    ids_ref, off_ref, x_hbm, lib_hbm, first_hbm, cos_hbm, sin_hbm, small_hbm, table_hbm, back_hbm,
    last_hbm, out_ref,
    x_ref, lib_ref, first_ref, cos_ref, sin_ref, small_ref, table_ref, back_ref, last_ref,
    real_ref, imag_ref, con_ref, halves_ref, pow_ref, pair_ref, sum_out, sum_in, total_ref,
    picks, parts, held, g_real, g_imag, g_energy, base_ref, power_ref, part_ref, mids, stat_ref,
    local_sem, pick_send, pick_recv, spread_send, spread_recv, gather_send, gather_recv,
    swap_send, swap_recv, pair_send, pair_recv, sum_send, sum_recv, done_send, done_recv,
    out_send, out_recv,
):
    tile = lax.axis_index("tile")
    orient = lax.axis_index("orient")
    core = lax.rem(orient, 2)
    chip = orient // 2
    n_chip = n_orient // 2
    steps, size = picks.shape[1], picks.shape[3]
    slots = lib_ref.shape[0]
    rows, length = real_ref.shape
    half, quarter = length // 2, length // 4
    partner = (tile, chip * 2 + 1 - core)
    tiles = [(lax.rem(tile + k, n_tile), orient) for k in range(1, n_tile)]
    chips = [(tile, lax.rem(chip + k, n_chip) * 2 + core) for k in range(1, n_chip)]
    strides = [1 << s for s in range((n_tile - 1).bit_length())]

    def local(at, src, dst):
        copy = pltpu.make_async_copy(src, dst, local_sem.at[at])
        copy.start()
        return copy

    loads = dict(
        lib=local(0, lib_hbm, lib_ref),
        x=local(1, x_hbm.at[core], x_ref),
        first=local(2, first_hbm, first_ref),
        cos=local(3, cos_hbm, cos_ref),
        sin=local(4, sin_hbm, sin_ref),
        small=local(5, small_hbm, small_ref),
        table=local(6, table_hbm, table_ref),
        back=local(7, back_hbm, back_ref),
        last=local(8, last_hbm, last_ref),
    )
    barrier = pltpu.get_barrier_semaphore()
    for device in [partner] + tiles + chips:
        pl.semaphore_signal(barrier, inc=1, device_id=device, device_id_type=MESH)

    def send(src, dst, send_sem, recv_sem, device):
        copy = pltpu.make_async_remote_copy(
            src_ref=src, dst_ref=dst, send_sem=send_sem, recv_sem=recv_sem,
            device_id=device, device_id_type=MESH,
        )
        copy.start()
        return copy

    strip = size // n_tile
    loads["lib"].wait()
    for step in range(steps):
        chosen = ids_ref[0, step]
        owner = chosen // slots
        picked = lib_ref[chosen - owner * slots, 0]
        keep = jnp.where(owner == tile, 1.0, 0.0).astype(f32)
        picked = jnp.where(keep > 0.0, picked.astype(f32), 0.0).astype(bf16)
        for q in range(n_tile):
            picks[q, step] = picked[q * strip : (q + 1) * strip]
    pl.semaphore_wait(barrier, 1 + len(tiles) + len(chips))
    pick_copies = [
        send(picks.at[device[0]], parts.at[k], pick_send.at[k], pick_recv.at[k], device)
        for k, device in enumerate(tiles)
    ]

    loads["x"].wait()
    loads["first"].wait()
    halves_ref[...] = dot(first_ref[...], x_ref[...]).astype(bf16)

    template = picks[tile].astype(f32)
    for k, copy in enumerate(pick_copies):
        copy.wait()
        template = template + parts[k].astype(f32)
    held[core, chip, tile] = template.astype(bf16)
    own = held.at[core, chip, tile]
    spread_copies = [
        send(own, own, spread_send.at[k], spread_recv.at[k], device)
        for k, device in enumerate(chips)
    ]

    def source(k):
        return lax.rem(chip + n_chip - k, n_chip)

    def gather(k):
        strip_ref = held.at[core, source(k), tile]
        return [
            send(strip_ref, strip_ref, gather_send.at[k, j], gather_recv.at[k, j], device)
            for j, device in enumerate(tiles)
        ]

    gathers = [gather(0)]

    loads["cos"].wait()
    loads["sin"].wait()
    sums = {}
    for which in range(2):
        side = core if which else 1 - core
        columns = pl.ds(pl.multiple_of(side * half, half), half)
        half_real, half_imag = halves_ref[:rows], halves_ref[rows:]
        cosine, sine = cos_ref[:, columns], sin_ref[:, columns]
        spec_real = dot(half_real, cosine) + dot(half_imag, sine)
        spec_imag = dot(half_imag, cosine) - dot(half_real, sine)
        real_ref[:, columns] = spec_real
        imag_ref[:, columns] = spec_imag
        power = spec_real * spec_real + spec_imag * spec_imag
        if which == 0:
            pow_ref[...] = power.astype(bf16)
            pair_copy = send(pow_ref, pair_ref, pair_send, pair_recv, partner)
        else:
            total_ref[core] = power
    for k in range(1, n_chip):
        spread_copies[k - 1].wait()
        gathers.append(gather(k))
    tile_contrast((off_ref[core, 0] - off_ref[core, 1]).astype(f32), con_ref)

    def across(s):
        up, down = strides[s], strides[-1 - s]
        other = [tile + d * (1 - 2 * lax.rem(tile // d, 2)) for d in (up, down)]
        return (other[0] * (1 - core) + other[1] * core, orient)

    def sum_step(s):
        sum_out[s] = total_ref[core].astype(bf16)
        return send(sum_out.at[s], sum_in.at[s], sum_send.at[s], sum_recv.at[s], across(s))

    pair_copy.wait()
    total_ref[core] = total_ref[core] + pair_ref[...].astype(f32)
    pending = [sum_step(0)]

    def sum_next():
        s = len(pending) - 1
        pending[s].wait()
        total_ref[core] = total_ref[core] + sum_in[s].astype(f32)
        if s + 1 < len(strides):
            pending.append(sum_step(s + 1))
        else:
            mine = total_ref.at[core]
            pending.append(send(mine, mine, done_send, done_recv, partner))

    batch = min(n_chip, 4)

    def spectra(which, place, at):
        images = held[which, place]
        images = jnp.concatenate([images[:, s].reshape(size, size) for s in range(steps)], axis=1)
        template_spectra(
            images, small_ref, table_ref, base_ref, power_ref, lambda n: steps * at + n
        )

    loads["small"].wait()
    loads["table"].wait()
    swaps = []
    for k in range(n_chip):
        for copy in gathers[k]:
            copy.wait()
        block = held.at[core, source(k)]
        swaps.append(send(block, block, swap_send.at[k], swap_recv.at[k], partner))
        if n_chip == batch:
            spectra(core, source(k), core * batch + source(k))
        if k % 2 == 1 and len(pending) <= len(strides):
            sum_next()
    while len(pending) <= len(strides):
        sum_next()
    for k in range(n_chip):
        swaps[k].wait()
        if n_chip == batch:
            spectra(1 - core, source(k), (1 - core) * batch + source(k))
    pending[-1].wait()
    tile_gains(
        n_tile * 2, total_ref, real_ref, imag_ref, con_ref, g_real, g_imag, g_energy
    )
    loads["back"].wait()
    loads["last"].wait()
    count = 2 * batch * steps
    rounds = n_chip // batch
    out_copies = []
    for turn in range(rounds):
        if n_chip != batch:
            def fill(i, carry):
                spectra(i // batch, turn * batch + lax.rem(i, batch), i)
                return carry

            lax.fori_loop(0, 2 * batch, fill, 0)

        def weigh(t, carry):
            energy(t, power_ref, g_energy, part_ref)
            return carry

        lax.fori_loop(0, count, weigh, 0)

        def visit(group, carry):
            for u in range(4):
                t = group * 4 + u
                column = pl.ds(pl.multiple_of(t * quarter, quarter), quarter)
                half_back(t, column, base_ref, back_ref, g_real, g_imag, mids)
            return carry

        lax.fori_loop(0, count // 4, visit, 0)
        scales = scales_of(part_ref, count)
        for k in range(valid // quarter):
            for n in range(count // 2):
                fresh = turn == 0 and n == 0
                statistics(k, n, fresh, scales[2 * n : 2 * n + 2], mids, last_ref, stat_ref.at[k])
            if turn == rounds - 1:
                found = finish((stat_ref[k, 0], stat_ref[k, 1], stat_ref[k, 2]), rounds * count)
                columns = slice(k * quarter, (k + 1) * quarter)
                for which in range(2):
                    out_ref[which, core, :, columns] = found[which].astype(bf16)
                    block = out_ref.at[which, core, :, columns]
                    sems = out_send.at[k, which], out_recv.at[k, which]
                    out_copies.append(send(block, block, *sems, partner))
    for copy in out_copies:
        copy.wait()


def body(n_tile, n_orient, micrograph_tiles, tile_offsets, library, orient_ids):
    tile_count, length = micrograph_tiles.shape[:2]
    slots, _, size, _ = library.shape
    steps = orient_ids.shape[1]
    n_chip = n_orient // 2
    assert tile_count == 2 and n_orient % 2 == 0 and n_tile & (n_tile - 1) == 0
    assert n_chip % min(n_chip, 4) == 0 and steps == 2
    half, quarter = length // 2, length // 4
    assert size == quarter and VALID % quarter == 0
    t = tables(length, size, VALID)
    rows = t["first"].shape[0] // 2
    names = ("first", "cos", "sin", "small", "base", "back", "last")
    count = 2 * min(n_chip, 4) * steps
    levels = (n_tile - 1).bit_length()
    strip = size // n_tile
    shape = jax.ShapeDtypeStruct
    vmem, dma = pltpu.VMEM, pltpu.SemaphoreType.DMA
    both = pl.pallas_call(
        functools.partial(search_kernel, n_tile, n_orient, VALID),
        out_shape=shape((2, 2, VALID, VALID), bf16),
        in_specs=[SMEM, SMEM] + [ANY] * 9,
        out_specs=VMEM,
        scratch_shapes=[
            vmem((length, length), bf16),
            vmem(library.shape, bf16),
            *[vmem(t[name].shape, bf16) for name in names],
            *[vmem((rows, length), f32)] * 3,
            vmem((2 * rows, length), bf16),
            vmem((rows, half), bf16),
            vmem((rows, half), bf16),
            vmem((levels, rows, half), bf16),
            vmem((levels, rows, half), bf16),
            vmem((2, rows, half), f32),
            vmem((n_tile, steps, strip, size), bf16),
            vmem((n_tile - 1, steps, strip, size), bf16),
            vmem((2, n_chip, n_tile, steps, strip, size), bf16),
            *[vmem((rows, length), bf16)] * 3,
            vmem((count, rows, 2 * length), bf16),
            vmem((count, rows, length), bf16),
            vmem((count, 8, quarter), f32),
            vmem((VALID // quarter, length, count * quarter), bf16),
            vmem((VALID // quarter, 3, VALID, quarter), f32),
            dma((9,)),
            dma((n_tile - 1,)),
            dma((n_tile - 1,)),
            dma((n_chip - 1,)),
            dma((n_chip - 1,)),
            dma((n_chip, n_tile - 1)),
            dma((n_chip, n_tile - 1)),
            dma((n_chip,)),
            dma((n_chip,)),
            dma, dma,
            dma((levels,)),
            dma((levels,)),
            dma, dma,
            dma((VALID // quarter, 2)),
            dma((VALID // quarter, 2)),
        ],
        compiler_params=pltpu.CompilerParams(
            collective_id=0, has_side_effects=True, vmem_limit_bytes=GRANT
        ),
    )(orient_ids, tile_offsets, micrograph_tiles, library, *[t[name] for name in names])
    return (both[0].astype(f32), both[1].astype(f32))


def solution(mesh):
    placed = (
        P("tile", None, None),
        P("tile", None),
        P("tile", "orient", None, None),
        P("orient", None),
    )
    return jax.shard_map(
        functools.partial(body, mesh.shape["tile"], mesh.shape["orient"]),
        mesh=mesh,
        in_specs=placed,
        out_specs=(P("tile", None, None), P("tile", None, None)),
        check_vma=False,
    )
```

```python
import functools
import math

import jax
import jax.numpy as jnp
import numpy as np
from jax import lax
from jax.experimental import pallas as pl
from jax.experimental.pallas import tpu as pltpu
from jax.sharding import PartitionSpec as P

VALID = 384
AMPLITUDE = 0.07
DEFOCUS_BASE = 100.0
DEFOCUS_TILT = 0.002
FLOOR_SHARE = 0.25
f32, bf16 = jnp.float32, jnp.bfloat16
MESH = pl.DeviceIdType.MESH
VMEM = pl.BlockSpec(memory_space=pltpu.VMEM)
HBM = pl.BlockSpec(memory_space=pltpu.HBM)
GRANT = 46 * 1024 * 1024


def tables(length, size, valid):
    half, quarter = length // 2, length // 4
    rows = -(-(half + 1) // 16) * 16
    b_index = np.concatenate([np.arange(0, half, 2), np.arange(1, half, 2), [half]])
    a_index = np.concatenate([np.arange(r, length, 4) for r in range(4)])
    j_index = np.arange(length)

    def wave(function, left, right):
        return function((left[:, None] * right[None, :]) % length * (2.0 * np.pi / length))

    first = np.zeros((2, rows, length))
    first[0, : half + 1] = wave(np.cos, b_index, j_index)
    first[1, : half + 1] = -wave(np.sin, b_index, j_index)
    cosine = wave(np.cos, j_index, a_index)
    sine = wave(np.sin, j_index, a_index)
    base, back = [], []
    for r in range(4):
        columns = slice(r * quarter, (r + 1) * quarter)
        c, s = cosine[:size, columns], sine[:size, columns]
        base.append((np.concatenate([c, s]), np.concatenate([-s, c])))
        c = wave(np.cos, a_index[columns], j_index[:quarter])
        s = wave(np.sin, a_index[columns], j_index[:quarter])
        back.append(np.block([[c, s], [-s, c]]))
    last = []
    for parity in range(2):
        b_part = b_index[parity * quarter : (parity + 1) * quarter]
        count = np.where(b_part == 0, 1.0, 2.0)
        c = wave(np.cos, j_index[:half], b_part) * count / length
        s = -wave(np.sin, j_index[:half], b_part) * count / length
        if parity == 0:
            s[:, 0] = np.cos(np.pi * j_index[:half]) / length
        last.append(np.concatenate([c, s], axis=1))

    def narrow(value):
        return np.asarray(value, np.float32).astype(jnp.bfloat16)

    first = first.reshape(2 * rows, length)
    return dict(
        first=narrow(first),
        small=narrow(np.ascontiguousarray(first[:, :size])),
        cos=narrow(cosine),
        sin=narrow(sine),
        base=narrow(np.concatenate([base[2 * p + q][w] for p in range(2) for w in range(2) for q in range(2)], axis=1)),
        back=narrow(np.stack(back)),
        last=narrow(np.stack(last)),
    )


def dot(left, right):
    return jnp.dot(left, right, preferred_element_type=jnp.float32)


def sine_of_turns(turns):
    part = turns - jnp.floor(turns + 0.5)
    mirrored = jnp.where(part > 0.0, 0.5, -0.5) - part
    part = jnp.where(jnp.abs(part) > 0.25, mirrored, part)
    angle = part * (2.0 * math.pi)
    square = angle * angle
    poly = -1.0 / 39916800.0
    for term in (1.0 / 362880.0, -1.0 / 5040.0, 1.0 / 120.0, -1.0 / 6.0, 1.0):
        poly = poly * square + term
    return angle * poly


def row_index(rows, half):
    row = lax.broadcasted_iota(jnp.int32, (rows, 1), 0)
    quarter = half // 2
    return row, jnp.where(row < quarter, 2 * row, jnp.where(row < half, 2 * row - half + 1, row))


def row_weight(rows, half):
    row, b_index = row_index(rows, half)
    single = (b_index == 0) | (row == half)
    return jnp.where(row > half, 0.0, jnp.where(single, 1.0, 2.0)).astype(f32)


def tile_contrast(tilt, real_ref, imag_ref, seen_real, seen_imag, seen_energy):
    rows, length = real_ref.shape
    half, quarter = length // 2, length // 4
    row, b_index = row_index(rows, half)
    b_index = jnp.where(row > half, 0, b_index).astype(f32) / length
    lane = lax.broadcasted_iota(jnp.int32, (1, length), 1)
    a_index = 4 * lax.rem(lane, quarter) + lane // quarter
    a_index = jnp.where(a_index < half, a_index, a_index - length).astype(f32) / length
    s2 = a_index * a_index + b_index * b_index
    defocus = DEFOCUS_BASE + DEFOCUS_TILT * tilt
    shift = math.asin(AMPLITUDE) / (2.0 * math.pi)
    contrast = -sine_of_turns(s2 * (0.5 * defocus) + shift)
    contrast = jnp.where(s2 > 0.0, contrast, 0.0)
    seen_real[...] = (real_ref[...] * contrast).astype(bf16)
    seen_imag[...] = (imag_ref[...] * contrast).astype(bf16)
    seen_energy[...] = (contrast * contrast * (row_weight(rows, half) / (length * length))).astype(bf16)


def template_spectra(
    images, small_ref, table_ref, seen_real, seen_imag, seen_energy, base_ref, power_ref, place
):
    rows = small_ref.shape[0] // 2
    size = images.shape[0]
    half = table_ref.shape[1] // 4
    halves = dot(small_ref[...], images).astype(bf16)
    for n in range(images.shape[1] // size):
        columns = slice(n * size, (n + 1) * size)
        joined = jnp.concatenate([halves[:rows, columns], halves[rows:, columns]], axis=1)
        for side in range(2):
            at = 2 * side * half
            columns = slice(side * half, (side + 1) * half)
            real = dot(joined, table_ref[:, at : at + half]).astype(bf16)
            imag = dot(joined, table_ref[:, at + half : at + 2 * half]).astype(bf16)
            left, right = seen_real[:, columns], seen_imag[:, columns]
            base_ref[place(n), :, at : at + half] = left * real + right * imag
            base_ref[place(n), :, at + half : at + 2 * half] = right * real - left * imag
            power_ref[place(n), :, columns] = (real * real + imag * imag) * seen_energy[:, columns]


def tile_gains(tiles, total_ref, gain_ref):
    rows, length = gain_ref.shape
    half = length // 2
    weight = row_weight(rows, half)
    mean = (jnp.sum(total_ref[0] * weight) + jnp.sum(total_ref[1] * weight)) / tiles
    floor = FLOOR_SHARE * (mean / (length * length))
    for side in range(2):
        columns = slice(side * half, (side + 1) * half)
        gain_ref[:, columns] = (1.0 / jnp.maximum(total_ref[side] / tiles, floor)).astype(bf16)


def energy(t, power_ref, gain_ref, part_ref):
    rows, length = gain_ref.shape
    share = power_ref[t] * gain_ref[...]
    share = share[:, : length // 2] + share[:, length // 2 :]
    total = None
    for row in range(0, rows, 16):
        piece = share[row : row + 8] + share[row + 8 : row + 16]
        piece = piece.astype(f32)
        total = piece if total is None else total + piece
    part_ref[t] = total[:, : length // 4] + total[:, length // 4 :]


def half_back(t, column, base_ref, back_ref, gain_ref, mids):
    rows, length = gain_ref.shape
    quarter = length // 4
    half = 2 * quarter
    found = []
    for side in range(2):
        columns = slice(side * half, (side + 1) * half)
        at = 2 * side * half
        gain = gain_ref[:, columns]
        prod_real = base_ref[t, :, at : at + half] * gain
        prod_imag = base_ref[t, :, at + half : at + 2 * half] * gain
        for q in range(2):
            part = slice(q * quarter, (q + 1) * quarter)
            joined = jnp.concatenate([prod_real[:, part], prod_imag[:, part]], axis=1)
            found.append(dot(joined, back_ref[2 * side + q]))
    plus02, minus02 = found[0] + found[2], found[0] - found[2]
    plus13, minus13 = found[1] + found[3], found[1] - found[3]
    real, imag = slice(0, quarter), slice(quarter, 2 * quarter)
    out = (
        (plus02[:, real] + plus13[:, real], plus02[:, imag] + plus13[:, imag]),
        (minus02[:, real] - minus13[:, imag], minus02[:, imag] + minus13[:, real]),
        (plus02[:, real] - plus13[:, real], plus02[:, imag] - plus13[:, imag]),
    )
    row = lax.broadcasted_iota(jnp.int32, (quarter, quarter), 0)
    for k, (mid_real, mid_imag) in enumerate(out):
        top = jnp.where(row == 0, mid_real[2 * quarter : 2 * quarter + 1], mid_imag[:quarter])
        mids[k, 0:quarter, column] = mid_real[:quarter].astype(bf16)
        mids[k, quarter : 2 * quarter, column] = top.astype(bf16)
        mids[k, 2 * quarter : 3 * quarter, column] = mid_real[quarter : 2 * quarter].astype(bf16)
        mids[k, 3 * quarter : 4 * quarter, column] = mid_imag[quarter : 2 * quarter].astype(bf16)


def scales_of(part_ref, count):
    return [lax.rsqrt(jnp.sum(part_ref[t]) + 1e-06) for t in range(count)]


def statistics(k, n, fresh, scales, mids, last_ref, stat_ref):
    quarter = last_ref.shape[1] // 2
    half = 2 * quarter
    columns = slice(n * half, (n + 1) * half)
    even = dot(last_ref[0], mids[k, :half, columns])
    odd = dot(last_ref[1], mids[k, half:, columns])
    one, two = scales
    for rows, (e, o) in ((slice(0, half), (even, odd)), (slice(half, half + quarter), (even[:quarter], -odd[:quarter]))):
        left = (e[:, :quarter] + o[:, :quarter]) * one
        right = (e[:, quarter:] + o[:, quarter:]) * two
        top, add, square = jnp.maximum(left, right), left + right, left * left + right * right
        if not fresh:
            top = jnp.maximum(stat_ref[0, rows], top)
            add = stat_ref[1, rows] + add
            square = stat_ref[2, rows] + square
        stat_ref[0, rows] = top
        stat_ref[1, rows] = add
        stat_ref[2, rows] = square


def finish(stats, searched):
    peak, add, squares = stats
    mean = add / searched
    variance = squares / searched - mean * mean
    return peak, (peak - mean) * lax.rsqrt(variance + 1e-06)


def flip(index, bits):
    at = 1
    while at <= bits:
        if bits & at:
            index = index + at * (1 - 2 * lax.rem(index // at, 2))
        at *= 2
    return index


def search_kernel(
    n_tile, n_orient, valid,
    ids_hbm, off_hbm, x_hbm, lib_hbm, first_hbm, cos_hbm, sin_hbm, small_hbm, table_hbm, back_hbm,
    last_hbm, out_ref,
    ids_ref, off_ref, x_ref, lib_ref, first_ref, cos_ref, sin_ref, small_ref, table_ref, back_ref, last_ref,
    real_ref, imag_ref, halves_ref, pow_ref, pair_ref, sum_out, sum_in, total_ref, picks, parts,
    held, seen_real, seen_imag, seen_energy, gain_ref, base_ref, power_ref, part_ref, mids, stat_ref,
    local_sem, pick_send, pick_recv, spread_send, spread_recv,
    swap_send, swap_recv, pair_send, pair_recv, sum_send, sum_recv, done_send, done_recv,
    out_send, out_recv,
):
    tile = lax.axis_index("tile")
    orient = lax.axis_index("orient")
    core = lax.rem(orient, 2)
    chip = orient // 2
    n_chip = n_orient // 2
    steps, size = picks.shape[0], picks.shape[1]
    slots = lib_ref.shape[0]
    rows, length = real_ref.shape
    half, quarter = length // 2, length // 4
    partner = (tile, chip * 2 + 1 - core)
    tiles = [(flip(tile, k), orient) for k in range(1, n_tile)]
    chips = [(tile, flip(chip, k) * 2 + core) for k in range(1, n_chip)]

    def local(at, src, dst):
        copy = pltpu.make_async_copy(src, dst, local_sem.at[at])
        copy.start()
        return copy

    loads = dict(
        ids=local(9, ids_hbm, ids_ref),
        off=local(10, off_hbm, off_ref),
        lib=local(0, lib_hbm, lib_ref),
        x=local(1, x_hbm.at[core], x_ref),
        first=local(2, first_hbm, first_ref),
        cos=local(3, cos_hbm, cos_ref),
        sin=local(4, sin_hbm, sin_ref),
        small=local(5, small_hbm, small_ref),
        table=local(6, table_hbm, table_ref),
        back=local(7, back_hbm, back_ref),
        last=local(8, last_hbm, last_ref),
    )
    barrier = pltpu.get_barrier_semaphore()
    for device in [partner] + tiles + chips:
        pl.semaphore_signal(barrier, inc=1, device_id=device, device_id_type=MESH)

    def send(src, dst, send_sem, recv_sem, device):
        copy = pltpu.make_async_remote_copy(
            src_ref=src, dst_ref=dst, send_sem=send_sem, recv_sem=recv_sem,
            device_id=device, device_id_type=MESH,
        )
        copy.start()
        return copy

    loads["ids"].wait()
    loads["lib"].wait()
    for step in range(steps):
        chosen = ids_ref[0, step]
        owner = chosen // slots
        picked = lib_ref[chosen - owner * slots, 0]
        keep = jnp.where(owner == tile, 1.0, 0.0).astype(f32)
        picks[step] = jnp.where(keep > 0.0, picked.astype(f32), 0.0).astype(bf16)
    loads["x"].wait()
    loads["first"].wait()
    halves_ref[...] = dot(first_ref[...], x_ref[...]).astype(bf16)

    pl.semaphore_wait(barrier, 1 + len(tiles) + len(chips))
    pick_copies = [
        send(picks, parts.at[k], pick_send.at[k], pick_recv.at[k], device)
        for k, device in enumerate(tiles)
    ]
    loads["cos"].wait()
    loads["sin"].wait()
    for which in range(2):
        side = core if which else 1 - core
        columns = pl.ds(pl.multiple_of(side * half, half), half)
        half_real, half_imag = halves_ref[:rows], halves_ref[rows:]
        cosine, sine = cos_ref[:, columns], sin_ref[:, columns]
        spec_real = dot(half_real, cosine) + dot(half_imag, sine)
        spec_imag = dot(half_imag, cosine) - dot(half_real, sine)
        real_ref[:, columns] = spec_real
        imag_ref[:, columns] = spec_imag
        power = spec_real * spec_real + spec_imag * spec_imag
        if which == 0:
            pow_ref[...] = power.astype(bf16)
            pair_copy = send(pow_ref, pair_ref, pair_send, pair_recv, partner)
        else:
            total_ref[core] = power
    pair_copy.wait()
    sum_out[...] = (total_ref[core] + pair_ref[...].astype(f32)).astype(bf16)
    sum_copies = [
        send(sum_out, sum_in.at[k], sum_send.at[k], sum_recv.at[k], device)
        for k, device in enumerate(tiles)
    ]

    def swap(k):
        block = held.at[core, flip(chip, k)]
        return send(block, block, swap_send.at[k], swap_recv.at[k], partner)

    template = picks[...].astype(f32)
    for k, copy in enumerate(pick_copies):
        copy.wait()
        template = template + parts[k].astype(f32)
    held[core, chip] = template.astype(bf16)
    own = held.at[core, chip]
    spread_copies = [
        send(own, own, spread_send.at[k], spread_recv.at[k], device)
        for k, device in enumerate(chips)
    ]
    swaps = [swap(0)]
    loads["off"].wait()
    tilt = (off_ref[core, 0] - off_ref[core, 1]).astype(f32)
    tile_contrast(tilt, real_ref, imag_ref, seen_real, seen_imag, seen_energy)

    batch = min(n_chip, 4)

    def spectra(which, place, at):
        images = held[which, place]
        images = jnp.concatenate([images[s] for s in range(steps)], axis=1)
        template_spectra(
            images, small_ref, table_ref, seen_real, seen_imag, seen_energy, base_ref, power_ref,
            lambda n: steps * at + n,
        )

    def early(which, k):
        if n_chip == batch:
            spectra(which, flip(chip, k), which * batch + flip(chip, k))

    loads["small"].wait()
    loads["table"].wait()
    early(core, 0)
    swaps[0].wait()
    early(1 - core, 0)
    total = sum_out[...].astype(f32)
    for k, copy in enumerate(sum_copies):
        copy.wait()
        total = total + sum_in[k].astype(f32)
    total_ref[core] = total
    mine = total_ref.at[core]
    done_copy = send(mine, mine, done_send, done_recv, partner)
    for k in range(1, n_chip):
        spread_copies[k - 1].wait()
        swaps.append(swap(k))
        early(core, k)
    for k in range(1, n_chip):
        swaps[k].wait()
        early(1 - core, k)
    done_copy.wait()
    tile_gains(n_tile * 2, total_ref, gain_ref)
    loads["back"].wait()
    loads["last"].wait()
    count = 2 * batch * steps
    rounds = n_chip // batch
    out_copies = []
    for turn in range(rounds):
        if n_chip != batch:
            def fill(i, carry):
                spectra(i // batch, turn * batch + lax.rem(i, batch), i)
                return carry

            lax.fori_loop(0, 2 * batch, fill, 0)

        def weigh(t, carry):
            energy(t, power_ref, gain_ref, part_ref)
            return carry

        lax.fori_loop(0, count, weigh, 0)

        def visit(group, carry):
            for u in range(4):
                t = group * 4 + u
                column = pl.ds(pl.multiple_of(t * quarter, quarter), quarter)
                half_back(t, column, base_ref, back_ref, gain_ref, mids)
            return carry

        lax.fori_loop(0, count // 4, visit, 0)
        scales = scales_of(part_ref, count)
        for k in range(valid // quarter):
            for n in range(count // 2):
                fresh = turn == 0 and n == 0
                statistics(k, n, fresh, scales[2 * n : 2 * n + 2], mids, last_ref, stat_ref.at[k])
            if turn == rounds - 1:
                found = finish((stat_ref[k, 0], stat_ref[k, 1], stat_ref[k, 2]), rounds * count)
                columns = slice(k * quarter, (k + 1) * quarter)
                for which in range(2):
                    out_ref[which, core, :, columns] = found[which].astype(bf16)
                    block = out_ref.at[which, core, :, columns]
                    sems = out_send.at[k, which], out_recv.at[k, which]
                    out_copies.append(send(block, block, *sems, partner))
    for copy in out_copies:
        copy.wait()


def body(n_tile, n_orient, micrograph_tiles, tile_offsets, library, orient_ids):
    tile_count, length = micrograph_tiles.shape[:2]
    slots, _, size, _ = library.shape
    steps = orient_ids.shape[1]
    n_chip = n_orient // 2
    assert tile_count == 2 and n_orient % 2 == 0 and n_tile & (n_tile - 1) == 0 and n_chip & (n_chip - 1) == 0
    assert n_chip % min(n_chip, 4) == 0 and steps == 2
    half, quarter = length // 2, length // 4
    assert size == quarter and VALID % quarter == 0
    t = tables(length, size, VALID)
    rows = t["first"].shape[0] // 2
    names = ("first", "cos", "sin", "small", "base", "back", "last")
    count = 2 * min(n_chip, 4) * steps
    shape = jax.ShapeDtypeStruct
    vmem, dma = pltpu.VMEM, pltpu.SemaphoreType.DMA
    operands = orient_ids, tile_offsets, micrograph_tiles, library, *[t[name] for name in names]
    both = pl.pallas_call(
        functools.partial(search_kernel, n_tile, n_orient, VALID),
        out_shape=shape((2, 2, VALID, VALID), bf16),
        in_specs=[HBM] * 11,
        out_specs=VMEM,
        scratch_shapes=[
            pltpu.SMEM(orient_ids.shape, jnp.int32),
            pltpu.SMEM(tile_offsets.shape, jnp.int32),
            vmem((length, length), bf16),
            vmem(library.shape, bf16),
            *[vmem(t[name].shape, bf16) for name in names],
            *[vmem((rows, length), f32)] * 2,
            vmem((2 * rows, length), bf16),
            *[vmem((rows, half), bf16)] * 3,
            vmem((n_tile - 1, rows, half), bf16),
            vmem((2, rows, half), f32),
            vmem((steps, size, size), bf16),
            vmem((n_tile - 1, steps, size, size), bf16),
            vmem((2, n_chip, steps, size, size), bf16),
            *[vmem((rows, length), bf16)] * 4,
            vmem((count, rows, 2 * length), bf16),
            vmem((count, rows, length), bf16),
            vmem((count, 8, quarter), f32),
            vmem((VALID // quarter, length, count * quarter), bf16),
            vmem((VALID // quarter, 3, VALID, quarter), f32),
            dma((11,)),
            dma((n_tile - 1,)),
            dma((n_tile - 1,)),
            dma((n_chip - 1,)),
            dma((n_chip - 1,)),
            dma((n_chip,)),
            dma((n_chip,)),
            dma, dma,
            dma((n_tile - 1,)),
            dma((n_tile - 1,)),
            dma, dma,
            dma((VALID // quarter, 2)),
            dma((VALID // quarter, 2)),
        ],
        compiler_params=pltpu.CompilerParams(
            collective_id=0, has_side_effects=True, vmem_limit_bytes=GRANT
        ),
    )(*[pltpu.with_memory_space_constraint(jnp.asarray(v), pltpu.HBM) for v in operands])
    return (both[0].astype(f32), both[1].astype(f32))


def solution(mesh):
    placed = (
        P("tile", None, None),
        P("tile", None),
        P("tile", "orient", None, None),
        P("orient", None),
    )
    return jax.shard_map(
        functools.partial(body, mesh.shape["tile"], mesh.shape["orient"]),
        mesh=mesh,
        in_specs=placed,
        out_specs=(P("tile", None, None), P("tile", None, None)),
        check_vma=False,
    )
```

```python
import functools
import math

import jax
import jax.numpy as jnp
import numpy as np
from jax import lax
from jax.experimental import pallas as pl
from jax.experimental.pallas import tpu as pltpu
from jax.sharding import PartitionSpec as P

VALID = 384
AMPLITUDE = 0.07
DEFOCUS_BASE = 100.0
DEFOCUS_TILT = 0.002
FLOOR_SHARE = 0.25
f32, bf16 = jnp.float32, jnp.bfloat16
MESH = pl.DeviceIdType.MESH
VMEM = pl.BlockSpec(memory_space=pltpu.VMEM)
HBM = pl.BlockSpec(memory_space=pltpu.HBM)
GRANT = 46 * 1024 * 1024


def tables(length, size, valid):
    half, quarter = length // 2, length // 4
    rows = -(-(half + 1) // 16) * 16
    b_index = np.concatenate([np.arange(0, half, 2), np.arange(1, half, 2), [half]])
    a_index = np.concatenate([np.arange(r, length, 4) for r in range(4)])
    j_index = np.arange(length)

    def wave(function, left, right):
        return function((left[:, None] * right[None, :]) % length * (2.0 * np.pi / length))

    first = np.zeros((2, rows, length))
    first[0, : half + 1] = wave(np.cos, b_index, j_index)
    first[1, : half + 1] = -wave(np.sin, b_index, j_index)
    cosine = wave(np.cos, j_index, a_index)
    sine = wave(np.sin, j_index, a_index)
    base, back = [], []
    for r in range(4):
        columns = slice(r * quarter, (r + 1) * quarter)
        c, s = cosine[:size, columns], sine[:size, columns]
        base.append((np.concatenate([c, s]), np.concatenate([-s, c])))
        c = wave(np.cos, a_index[columns], j_index[:quarter])
        s = wave(np.sin, a_index[columns], j_index[:quarter])
        back.append(np.block([[c, s], [-s, c]]))
    last = []
    for parity in range(2):
        b_part = b_index[parity * quarter : (parity + 1) * quarter]
        count = np.where(b_part == 0, 1.0, 2.0)
        c = wave(np.cos, j_index[:half], b_part) * count / length
        s = -wave(np.sin, j_index[:half], b_part) * count / length
        if parity == 0:
            s[:, 0] = np.cos(np.pi * j_index[:half]) / length
        last.append(np.concatenate([c, s], axis=1))

    def narrow(value):
        return np.asarray(value, np.float32).astype(jnp.bfloat16)

    first = first.reshape(2 * rows, length)
    return dict(
        first=narrow(first),
        small=narrow(np.ascontiguousarray(first[:, :size])),
        cos=narrow(cosine),
        sin=narrow(sine),
        base=narrow(np.concatenate([base[2 * p + q][w] for p in range(2) for w in range(2) for q in range(2)], axis=1)),
        back=narrow(np.stack(back)),
        last=narrow(np.stack(last)),
    )


def dot(left, right):
    return jnp.dot(left, right, preferred_element_type=jnp.float32)


def sine_of_turns(turns):
    part = turns - jnp.floor(turns + 0.5)
    mirrored = jnp.where(part > 0.0, 0.5, -0.5) - part
    part = jnp.where(jnp.abs(part) > 0.25, mirrored, part)
    angle = part * (2.0 * math.pi)
    square = angle * angle
    poly = -1.0 / 39916800.0
    for term in (1.0 / 362880.0, -1.0 / 5040.0, 1.0 / 120.0, -1.0 / 6.0, 1.0):
        poly = poly * square + term
    return angle * poly


def row_index(rows, half):
    row = lax.broadcasted_iota(jnp.int32, (rows, 1), 0)
    quarter = half // 2
    return row, jnp.where(row < quarter, 2 * row, jnp.where(row < half, 2 * row - half + 1, row))


def row_weight(rows, half):
    row, b_index = row_index(rows, half)
    single = (b_index == 0) | (row == half)
    return jnp.where(row > half, 0.0, jnp.where(single, 1.0, 2.0)).astype(f32)


def tile_contrast(tilt, real_ref, imag_ref, seen_real, seen_imag, seen_energy):
    rows, length = real_ref.shape
    half, quarter = length // 2, length // 4
    row, b_index = row_index(rows, half)
    b_index = jnp.where(row > half, 0, b_index).astype(f32) / length
    lane = lax.broadcasted_iota(jnp.int32, (1, length), 1)
    a_index = 4 * lax.rem(lane, quarter) + lane // quarter
    a_index = jnp.where(a_index < half, a_index, a_index - length).astype(f32) / length
    s2 = a_index * a_index + b_index * b_index
    defocus = DEFOCUS_BASE + DEFOCUS_TILT * tilt
    shift = math.asin(AMPLITUDE) / (2.0 * math.pi)
    contrast = -sine_of_turns(s2 * (0.5 * defocus) + shift)
    contrast = jnp.where(s2 > 0.0, contrast, 0.0)
    seen_real[...] = (real_ref[...] * contrast).astype(bf16)
    seen_imag[...] = (imag_ref[...] * contrast).astype(bf16)
    seen_energy[...] = (contrast * contrast * (row_weight(rows, half) / (length * length))).astype(bf16)


def template_spectra(
    images, small_ref, table_ref, seen_real, seen_imag, seen_energy, base_ref, power_ref, place
):
    rows = small_ref.shape[0] // 2
    size = images.shape[0]
    half = table_ref.shape[1] // 4
    halves = dot(small_ref[...], images).astype(bf16)
    for n in range(images.shape[1] // size):
        columns = slice(n * size, (n + 1) * size)
        joined = jnp.concatenate([halves[:rows, columns], halves[rows:, columns]], axis=1)
        for side in range(2):
            at = 2 * side * half
            columns = slice(side * half, (side + 1) * half)
            real = dot(joined, table_ref[:, at : at + half]).astype(bf16)
            imag = dot(joined, table_ref[:, at + half : at + 2 * half]).astype(bf16)
            left, right = seen_real[:, columns], seen_imag[:, columns]
            base_ref[place(n), :, at : at + half] = left * real + right * imag
            base_ref[place(n), :, at + half : at + 2 * half] = right * real - left * imag
            power_ref[place(n), :, columns] = (real * real + imag * imag) * seen_energy[:, columns]


def tile_gains(tiles, total_ref, gain_ref):
    rows, length = gain_ref.shape
    half = length // 2
    weight = row_weight(rows, half)
    mean = (jnp.sum(total_ref[0] * weight) + jnp.sum(total_ref[1] * weight)) / tiles
    floor = FLOOR_SHARE * (mean / (length * length))
    for side in range(2):
        columns = slice(side * half, (side + 1) * half)
        gain_ref[:, columns] = (1.0 / jnp.maximum(total_ref[side] / tiles, floor)).astype(bf16)


def energy(t, power_ref, gain_ref, part_ref):
    rows, length = gain_ref.shape
    share = power_ref[t] * gain_ref[...]
    share = share[:, : length // 2] + share[:, length // 2 :]
    total = None
    for row in range(0, rows, 16):
        piece = share[row : row + 8] + share[row + 8 : row + 16]
        piece = piece.astype(f32)
        total = piece if total is None else total + piece
    part_ref[t] = total[:, : length // 4] + total[:, length // 4 :]


def half_back(t, column, base_ref, back_ref, gain_ref, mids):
    rows, length = gain_ref.shape
    quarter = length // 4
    half = 2 * quarter
    found = []
    for side in range(2):
        columns = slice(side * half, (side + 1) * half)
        at = 2 * side * half
        gain = gain_ref[:, columns]
        prod_real = base_ref[t, :, at : at + half] * gain
        prod_imag = base_ref[t, :, at + half : at + 2 * half] * gain
        for q in range(2):
            part = slice(q * quarter, (q + 1) * quarter)
            joined = jnp.concatenate([prod_real[:, part], prod_imag[:, part]], axis=1)
            found.append(dot(joined, back_ref[2 * side + q]))
    plus02, minus02 = found[0] + found[2], found[0] - found[2]
    plus13, minus13 = found[1] + found[3], found[1] - found[3]
    real, imag = slice(0, quarter), slice(quarter, 2 * quarter)
    out = (
        (plus02[:, real] + plus13[:, real], plus02[:, imag] + plus13[:, imag]),
        (minus02[:, real] - minus13[:, imag], minus02[:, imag] + minus13[:, real]),
        (plus02[:, real] - plus13[:, real], plus02[:, imag] - plus13[:, imag]),
    )
    row = lax.broadcasted_iota(jnp.int32, (quarter, quarter), 0)
    for k, (mid_real, mid_imag) in enumerate(out):
        top = jnp.where(row == 0, mid_real[2 * quarter : 2 * quarter + 1], mid_imag[:quarter])
        mids[k, 0:quarter, column] = mid_real[:quarter].astype(bf16)
        mids[k, quarter : 2 * quarter, column] = top.astype(bf16)
        mids[k, 2 * quarter : 3 * quarter, column] = mid_real[quarter : 2 * quarter].astype(bf16)
        mids[k, 3 * quarter : 4 * quarter, column] = mid_imag[quarter : 2 * quarter].astype(bf16)


def scales_of(part_ref, count):
    return [lax.rsqrt(jnp.sum(part_ref[t]) + 1e-06) for t in range(count)]


def statistics(k, first, fresh, scales, mids, last_ref, stat_ref):
    quarter = last_ref.shape[1] // 2
    half = 2 * quarter
    columns = slice(first * quarter, (first + len(scales)) * quarter)
    even = dot(last_ref[0], mids[k, :half, columns])
    odd = dot(last_ref[1], mids[k, half:, columns])
    for rows, sign in ((slice(0, half), 1), (slice(half, half + quarter), -1)):
        top = add = square = None
        for n, scale in enumerate(scales):
            e = even[: rows.stop - rows.start, n * quarter : (n + 1) * quarter]
            o = odd[: rows.stop - rows.start, n * quarter : (n + 1) * quarter]
            score = (e + o if sign > 0 else e - o) * scale
            top = score if n == 0 else jnp.maximum(top, score)
            add = score if n == 0 else add + score
            square = score * score if n == 0 else square + score * score
        if not fresh:
            top = jnp.maximum(stat_ref[0, rows], top)
            add = stat_ref[1, rows] + add
            square = stat_ref[2, rows] + square
        stat_ref[0, rows] = top
        stat_ref[1, rows] = add
        stat_ref[2, rows] = square


def finish(stats, searched):
    peak, add, squares = stats
    mean = add / searched
    variance = squares / searched - mean * mean
    return peak, (peak - mean) * lax.rsqrt(variance + 1e-06)


def flip(index, bits):
    at = 1
    while at <= bits:
        if bits & at:
            index = index + at * (1 - 2 * lax.rem(index // at, 2))
        at *= 2
    return index


def flip_by(index, bits, count):
    flipped, at = 0, 1
    while at < count:
        one, other = lax.rem(index // at, 2), lax.rem(bits // at, 2)
        flipped = flipped + at * (one + other - 2 * one * other)
        at *= 2
    return flipped


def search_kernel(
    n_tile, n_orient, valid,
    ids_hbm, off_hbm, x_hbm, lib_hbm, first_hbm, cos_hbm, sin_hbm, small_hbm, table_hbm, back_hbm,
    last_hbm, out_ref,
    ids_ref, off_ref, x_ref, lib_ref, first_ref, cos_ref, sin_ref, small_ref, table_ref, back_ref, last_ref,
    real_ref, imag_ref, halves_ref, pow_ref, pair_ref, sum_out, sum_in, total_ref, picks, parts,
    held, seen_real, seen_imag, seen_energy, gain_ref, base_ref, power_ref, part_ref, mids, stat_ref,
    local_sem, pick_send, pick_recv, spread_send, spread_recv,
    swap_send, swap_recv, pair_send, pair_recv, sum_send, sum_recv, done_send, done_recv,
    out_send, out_recv,
):
    tile = lax.axis_index("tile")
    orient = lax.axis_index("orient")
    core = lax.rem(orient, 2)
    chip = orient // 2
    n_chip = n_orient // 2
    steps, size = picks.shape[0], picks.shape[1]
    slots = lib_ref.shape[0]
    rows, length = real_ref.shape
    half, quarter = length // 2, length // 4
    partner = (tile, chip * 2 + 1 - core)
    tiles = [(flip(tile, k), orient) for k in range(1, n_tile)]
    chips = [(tile, flip(chip, k) * 2 + core) for k in range(1, n_chip)]

    def local(at, src, dst):
        copy = pltpu.make_async_copy(src, dst, local_sem.at[at])
        copy.start()
        return copy

    loads = dict(
        ids=local(9, ids_hbm, ids_ref),
        off=local(10, off_hbm, off_ref),
        lib=local(0, lib_hbm, lib_ref),
        x=local(1, x_hbm.at[core], x_ref),
        first=local(2, first_hbm, first_ref),
        cos=local(3, cos_hbm, cos_ref),
        sin=local(4, sin_hbm, sin_ref),
    )
    barrier = pltpu.get_barrier_semaphore()
    for device in [partner] + tiles + chips:
        pl.semaphore_signal(barrier, inc=1, device_id=device, device_id_type=MESH)

    def send(src, dst, send_sem, recv_sem, device):
        copy = pltpu.make_async_remote_copy(
            src_ref=src, dst_ref=dst, send_sem=send_sem, recv_sem=recv_sem,
            device_id=device, device_id_type=MESH,
        )
        copy.start()
        return copy

    loads["ids"].wait()
    loads["lib"].wait()
    for step in range(steps):
        chosen = ids_ref[0, step]
        owner = chosen // slots
        picked = lib_ref[chosen - owner * slots, 0]
        keep = jnp.where(owner == tile, 1.0, 0.0).astype(f32)
        picks[step] = jnp.where(keep > 0.0, picked.astype(f32), 0.0).astype(bf16)
    pl.semaphore_wait(barrier, 1 + len(tiles) + len(chips))
    pick_copies = [
        send(picks, parts.at[k], pick_send.at[k], pick_recv.at[k], device)
        for k, device in enumerate(tiles)
    ]
    loads["x"].wait()
    loads["first"].wait()
    halves_ref[...] = dot(first_ref[...], x_ref[...]).astype(bf16)

    loads["cos"].wait()
    loads["sin"].wait()
    loads.update(
        small=local(5, small_hbm, small_ref),
        table=local(6, table_hbm, table_ref),
        back=local(7, back_hbm, back_ref),
        last=local(8, last_hbm, last_ref),
    )
    for which in range(2):
        side = core if which else 1 - core
        columns = pl.ds(pl.multiple_of(side * half, half), half)
        half_real, half_imag = halves_ref[:rows], halves_ref[rows:]
        cosine, sine = cos_ref[:, columns], sin_ref[:, columns]
        spec_real = dot(half_real, cosine) + dot(half_imag, sine)
        spec_imag = dot(half_imag, cosine) - dot(half_real, sine)
        real_ref[:, columns] = spec_real
        imag_ref[:, columns] = spec_imag
        power = spec_real * spec_real + spec_imag * spec_imag
        if which == 0:
            pow_ref[...] = power.astype(bf16)
            pair_copy = send(pow_ref, pair_ref, pair_send, pair_recv, partner)
        else:
            total_ref[core] = power
    levels = sum_in.shape[0]
    cut = (rows // 32) * 16
    pieces = [pl.ds(0, cut), pl.ds(cut, rows - cut)]
    sums = {}

    def sum_step(s, piece):
        up, down = flip(tile, 1 << s), flip(tile, 1 << (levels - 1 - s))
        device = (up * (1 - core) + down * core, orient)
        at = s, pieces[piece]
        sum_out[at] = total_ref[core, pieces[piece]].astype(bf16)
        sems = sum_send.at[s, piece], sum_recv.at[s, piece]
        sums[s, piece] = send(sum_out.at[at], sum_in.at[at], *sems, device)

    def sum_wait(s, piece):
        sums[s, piece].wait()
        at = core, pieces[piece]
        total_ref[at] = total_ref[at] + sum_in[s, pieces[piece]].astype(f32)

    pair_copy.wait()
    for piece in range(2):
        at = core, pieces[piece]
        total_ref[at] = total_ref[at] + pair_ref[pieces[piece]].astype(f32)
        sum_step(0, piece)

    def swap(k):
        block = held.at[core, flip(chip, k)]
        return send(block, block, swap_send.at[k], swap_recv.at[k], partner)

    template = picks[...].astype(f32)
    for k, copy in enumerate(pick_copies):
        copy.wait()
        template = template + parts[k].astype(f32)
    held[core, chip] = template.astype(bf16)
    own = held.at[core, chip]
    spread_copies = [
        send(own, own, spread_send.at[k], spread_recv.at[k], device)
        for k, device in enumerate(chips)
    ]
    swaps = [swap(0)]
    loads["off"].wait()
    tilt = (off_ref[core, 0] - off_ref[core, 1]).astype(f32)
    tile_contrast(tilt, real_ref, imag_ref, seen_real, seen_imag, seen_energy)

    batch = min(n_chip, 4)

    def spectra(which, place, at):
        images = held[which, place]
        images = jnp.concatenate([images[s] for s in range(steps)], axis=1)
        template_spectra(
            images, small_ref, table_ref, seen_real, seen_imag, seen_energy, base_ref, power_ref,
            lambda n: steps * at + n,
        )

    def early(which, k):
        if n_chip == batch:
            spectra(which, flip(chip, k), which * batch + flip(chip, k))

    loads["small"].wait()
    loads["table"].wait()
    for s in range(1, levels):
        for piece in range(2):
            sum_wait(s - 1, piece)
            sum_step(s, piece)
            if s == 1 and piece == 0:
                early(core, 0)
    swaps[0].wait()
    early(1 - core, 0)
    done_copies = []
    for piece in range(2):
        sum_wait(levels - 1, piece)
        mine = total_ref.at[core, pieces[piece]]
        done_copies.append(send(mine, mine, done_send.at[piece], done_recv.at[piece], partner))
    ready = (n_chip + 1) // 2
    for k in range(1, ready):
        spread_copies[k - 1].wait()
        swaps.append(swap(k))
        early(core, k)
    for copy in done_copies:
        copy.wait()
    tile_gains(n_tile * 2, total_ref, gain_ref)
    for k in range(1, ready):
        swaps[k].wait()
        early(1 - core, k)
    loads["back"].wait()
    loads["last"].wait()

    def search(begin, end):
        def visit(k, carry):
            place = flip_by(chip, k, batch) if n_chip == batch else k
            for which in range(2):
                for step in range(steps):
                    t = (which * batch + place) * steps + step
                    column = pl.ds(pl.multiple_of(t * quarter, quarter), quarter)
                    energy(t, power_ref, gain_ref, part_ref)
                    half_back(t, column, base_ref, back_ref, gain_ref, mids)
            return carry

        lax.fori_loop(begin, end, visit, 0)

    if n_chip == batch:
        search(0, ready)
    for k in range(ready, n_chip):
        spread_copies[k - 1].wait()
        swaps.append(swap(k))
    for k in range(ready, n_chip):
        early(core, k)
    for k in range(ready, n_chip):
        swaps[k].wait()
        early(1 - core, k)
    count = 2 * batch * steps
    rounds = n_chip // batch
    out_copies = []
    for turn in range(rounds):
        if n_chip != batch:
            def fill(i, carry):
                spectra(i // batch, turn * batch + lax.rem(i, batch), i)
                return carry

            lax.fori_loop(0, 2 * batch, fill, 0)

        search(ready if n_chip == batch else 0, batch)
        scales = scales_of(part_ref, count)
        for k in range(valid // quarter):
            for n in range(0, count, 2):
                fresh = turn == 0 and n == 0
                statistics(k, n, fresh, scales[n : n + 2], mids, last_ref, stat_ref.at[k])
            if turn == rounds - 1:
                found = finish((stat_ref[k, 0], stat_ref[k, 1], stat_ref[k, 2]), rounds * count)
                columns = slice(k * quarter, (k + 1) * quarter)
                for which in range(2):
                    out_ref[which, core, :, columns] = found[which].astype(bf16)
                    block = out_ref.at[which, core, :, columns]
                    sems = out_send.at[k, which], out_recv.at[k, which]
                    out_copies.append(send(block, block, *sems, partner))
    for copy in out_copies:
        copy.wait()


def body(n_tile, n_orient, micrograph_tiles, tile_offsets, library, orient_ids):
    tile_count, length = micrograph_tiles.shape[:2]
    slots, _, size, _ = library.shape
    steps = orient_ids.shape[1]
    n_chip = n_orient // 2
    assert tile_count == 2 and n_orient % 2 == 0 and n_tile & (n_tile - 1) == 0 and n_chip & (n_chip - 1) == 0
    assert n_chip % min(n_chip, 4) == 0 and steps == 2
    half, quarter = length // 2, length // 4
    assert size == quarter and VALID % quarter == 0
    t = tables(length, size, VALID)
    rows = t["first"].shape[0] // 2
    names = ("first", "cos", "sin", "small", "base", "back", "last")
    count = 2 * min(n_chip, 4) * steps
    levels = (n_tile - 1).bit_length()
    shape = jax.ShapeDtypeStruct
    vmem, dma = pltpu.VMEM, pltpu.SemaphoreType.DMA
    operands = orient_ids, tile_offsets, micrograph_tiles, library, *[t[name] for name in names]
    both = pl.pallas_call(
        functools.partial(search_kernel, n_tile, n_orient, VALID),
        out_shape=shape((2, 2, VALID, VALID), bf16),
        in_specs=[HBM] * 11,
        out_specs=VMEM,
        scratch_shapes=[
            pltpu.SMEM(orient_ids.shape, jnp.int32),
            pltpu.SMEM(tile_offsets.shape, jnp.int32),
            vmem((length, length), bf16),
            vmem(library.shape, bf16),
            *[vmem(t[name].shape, bf16) for name in names],
            *[vmem((rows, length), f32)] * 2,
            vmem((2 * rows, length), bf16),
            *[vmem((rows, half), bf16)] * 2,
            *[vmem((levels, rows, half), bf16)] * 2,
            vmem((2, rows, half), f32),
            vmem((steps, size, size), bf16),
            vmem((n_tile - 1, steps, size, size), bf16),
            vmem((2, n_chip, steps, size, size), bf16),
            *[vmem((rows, length), bf16)] * 4,
            vmem((count, rows, 2 * length), bf16),
            vmem((count, rows, length), bf16),
            vmem((count, 8, quarter), f32),
            vmem((VALID // quarter, length, count * quarter), bf16),
            vmem((VALID // quarter, 3, VALID, quarter), f32),
            dma((11,)),
            dma((n_tile - 1,)),
            dma((n_tile - 1,)),
            dma((n_chip - 1,)),
            dma((n_chip - 1,)),
            dma((n_chip,)),
            dma((n_chip,)),
            dma, dma,
            dma((levels, 2)),
            dma((levels, 2)),
            dma((2,)),
            dma((2,)),
            dma((VALID // quarter, 2)),
            dma((VALID // quarter, 2)),
        ],
        compiler_params=pltpu.CompilerParams(
            collective_id=0, has_side_effects=True, vmem_limit_bytes=GRANT
        ),
    )(*[pltpu.with_memory_space_constraint(jnp.asarray(v), pltpu.HBM) for v in operands])
    return (both[0].astype(f32), both[1].astype(f32))


def solution(mesh):
    placed = (
        P("tile", None, None),
        P("tile", None),
        P("tile", "orient", None, None),
        P("orient", None),
    )
    return jax.shard_map(
        functools.partial(body, mesh.shape["tile"], mesh.shape["orient"]),
        mesh=mesh,
        in_specs=placed,
        out_specs=(P("tile", None, None), P("tile", None, None)),
        check_vma=False,
    )
```

```python
import functools
import math

import jax
import jax.numpy as jnp
import numpy as np
from jax import lax
from jax.experimental import pallas as pl
from jax.experimental.pallas import tpu as pltpu
from jax.sharding import PartitionSpec as P

VALID = 384
AMPLITUDE = 0.07
DEFOCUS_BASE = 100.0
DEFOCUS_TILT = 0.002
FLOOR_SHARE = 0.25
f32, bf16 = jnp.float32, jnp.bfloat16
MESH = pl.DeviceIdType.MESH
VMEM = pl.BlockSpec(memory_space=pltpu.VMEM)
HBM = pl.BlockSpec(memory_space=pltpu.HBM)
GRANT = 46 * 1024 * 1024


def tables(length, size, valid):
    half, quarter = length // 2, length // 4
    rows = -(-(half + 1) // 16) * 16
    b_index = np.concatenate([np.arange(0, half, 2), np.arange(1, half, 2), [half]])
    a_index = np.concatenate([np.arange(r, length, 4) for r in range(4)])
    j_index = np.arange(length)

    def wave(function, left, right):
        return function((left[:, None] * right[None, :]) % length * (2.0 * np.pi / length))

    first = np.zeros((2, rows, length))
    first[0, : half + 1] = wave(np.cos, b_index, j_index)
    first[1, : half + 1] = -wave(np.sin, b_index, j_index)
    cosine = wave(np.cos, j_index, a_index)
    sine = wave(np.sin, j_index, a_index)
    base, back = [], []
    for r in range(4):
        columns = slice(r * quarter, (r + 1) * quarter)
        c, s = cosine[:size, columns], sine[:size, columns]
        base.append((np.concatenate([c, s]), np.concatenate([-s, c])))
        c = wave(np.cos, a_index[columns], j_index[:quarter])
        s = wave(np.sin, a_index[columns], j_index[:quarter])
        back.append(np.block([[c, s], [-s, c]]))
    last = []
    for parity in range(2):
        b_part = b_index[parity * quarter : (parity + 1) * quarter]
        count = np.where(b_part == 0, 1.0, 2.0)
        c = wave(np.cos, j_index[:half], b_part) * count / length
        s = -wave(np.sin, j_index[:half], b_part) * count / length
        if parity == 0:
            s[:, 0] = np.cos(np.pi * j_index[:half]) / length
        last.append(np.concatenate([c, s], axis=1))

    def narrow(value):
        return np.asarray(value, np.float32).astype(jnp.bfloat16)

    first = first.reshape(2 * rows, length)
    return dict(
        first=narrow(first),
        small=narrow(np.ascontiguousarray(first[:, :size])),
        cos=narrow(cosine),
        sin=narrow(sine),
        base=narrow(np.concatenate([base[2 * p + q][w] for p in range(2) for w in range(2) for q in range(2)], axis=1)),
        back=narrow(np.stack(back)),
        last=narrow(np.stack(last)),
    )


def dot(left, right):
    return jnp.dot(left, right, preferred_element_type=jnp.float32)


def sine_of_turns(turns):
    part = turns - jnp.floor(turns + 0.5)
    mirrored = jnp.where(part > 0.0, 0.5, -0.5) - part
    part = jnp.where(jnp.abs(part) > 0.25, mirrored, part)
    angle = part * (2.0 * math.pi)
    square = angle * angle
    poly = -1.0 / 39916800.0
    for term in (1.0 / 362880.0, -1.0 / 5040.0, 1.0 / 120.0, -1.0 / 6.0, 1.0):
        poly = poly * square + term
    return angle * poly


def row_index(rows, half):
    row = lax.broadcasted_iota(jnp.int32, (rows, 1), 0)
    quarter = half // 2
    return row, jnp.where(row < quarter, 2 * row, jnp.where(row < half, 2 * row - half + 1, row))


def row_weight(rows, half):
    row, b_index = row_index(rows, half)
    single = (b_index == 0) | (row == half)
    return jnp.where(row > half, 0.0, jnp.where(single, 1.0, 2.0)).astype(f32)


def tile_contrast(tilt, real_ref, imag_ref, seen_real, seen_imag, seen_energy):
    rows, length = real_ref.shape
    half, quarter = length // 2, length // 4
    row, b_index = row_index(rows, half)
    b_index = jnp.where(row > half, 0, b_index).astype(f32) / length
    lane = lax.broadcasted_iota(jnp.int32, (1, length), 1)
    a_index = 4 * lax.rem(lane, quarter) + lane // quarter
    a_index = jnp.where(a_index < half, a_index, a_index - length).astype(f32) / length
    s2 = a_index * a_index + b_index * b_index
    defocus = DEFOCUS_BASE + DEFOCUS_TILT * tilt
    shift = math.asin(AMPLITUDE) / (2.0 * math.pi)
    contrast = -sine_of_turns(s2 * (0.5 * defocus) + shift)
    contrast = jnp.where(s2 > 0.0, contrast, 0.0)
    seen_real[...] = (real_ref[...] * contrast).astype(bf16)
    seen_imag[...] = (imag_ref[...] * contrast).astype(bf16)
    seen_energy[...] = (contrast * contrast * (row_weight(rows, half) / (length * length))).astype(bf16)


def template_spectra(
    images, small_ref, table_ref, seen_real, seen_imag, seen_energy, base_ref, power_ref, place
):
    rows = small_ref.shape[0] // 2
    size = images.shape[0]
    half = table_ref.shape[1] // 4
    halves = dot(small_ref[...], images).astype(bf16)
    for n in range(images.shape[1] // size):
        columns = slice(n * size, (n + 1) * size)
        joined = jnp.concatenate([halves[:rows, columns], halves[rows:, columns]], axis=1)
        for side in range(2):
            at = 2 * side * half
            columns = slice(side * half, (side + 1) * half)
            real = dot(joined, table_ref[:, at : at + half]).astype(bf16)
            imag = dot(joined, table_ref[:, at + half : at + 2 * half]).astype(bf16)
            power = real * real + imag * imag
            for which in range(seen_real.shape[0]):
                slot = place(which, n)
                left, right = seen_real[which, :, columns], seen_imag[which, :, columns]
                base_ref[slot, :, at : at + half] = left * real + right * imag
                base_ref[slot, :, at + half : at + 2 * half] = right * real - left * imag
                power_ref[slot, :, columns] = power * seen_energy[which, :, columns]


def tile_gains(tiles, total_ref, gain_ref):
    rows, length = gain_ref.shape
    half = length // 2
    weight = row_weight(rows, half)
    mean = (jnp.sum(total_ref[0] * weight) + jnp.sum(total_ref[1] * weight)) / tiles
    floor = FLOOR_SHARE * (mean / (length * length))
    for side in range(2):
        columns = slice(side * half, (side + 1) * half)
        gain_ref[:, columns] = (1.0 / jnp.maximum(total_ref[side] / tiles, floor)).astype(bf16)


def energy(t, power_ref, gain_ref, part_ref):
    rows, length = gain_ref.shape
    share = power_ref[t] * gain_ref[...]
    share = share[:, : length // 2] + share[:, length // 2 :]
    total = None
    for row in range(0, rows, 16):
        piece = share[row : row + 8] + share[row + 8 : row + 16]
        piece = piece.astype(f32)
        total = piece if total is None else total + piece
    part_ref[t] = total[:, : length // 4] + total[:, length // 4 :]


def half_back(t, column, base_ref, back_ref, gain_ref, mids):
    rows, length = gain_ref.shape
    quarter = length // 4
    half = 2 * quarter
    found = []
    for side in range(2):
        columns = slice(side * half, (side + 1) * half)
        at = 2 * side * half
        gain = gain_ref[:, columns]
        prod_real = base_ref[t, :, at : at + half] * gain
        prod_imag = base_ref[t, :, at + half : at + 2 * half] * gain
        for q in range(2):
            part = slice(q * quarter, (q + 1) * quarter)
            joined = jnp.concatenate([prod_real[:, part], prod_imag[:, part]], axis=1)
            found.append(dot(joined, back_ref[2 * side + q]))
    plus02, minus02 = found[0] + found[2], found[0] - found[2]
    plus13, minus13 = found[1] + found[3], found[1] - found[3]
    real, imag = slice(0, quarter), slice(quarter, 2 * quarter)
    out = (
        (plus02[:, real] + plus13[:, real], plus02[:, imag] + plus13[:, imag]),
        (minus02[:, real] - minus13[:, imag], minus02[:, imag] + minus13[:, real]),
        (plus02[:, real] - plus13[:, real], plus02[:, imag] - plus13[:, imag]),
    )
    row = lax.broadcasted_iota(jnp.int32, (quarter, quarter), 0)
    for k, (mid_real, mid_imag) in enumerate(out):
        top = jnp.where(row == 0, mid_real[2 * quarter : 2 * quarter + 1], mid_imag[:quarter])
        mids[k, 0:quarter, column] = mid_real[:quarter].astype(bf16)
        mids[k, quarter : 2 * quarter, column] = top.astype(bf16)
        mids[k, 2 * quarter : 3 * quarter, column] = mid_real[quarter : 2 * quarter].astype(bf16)
        mids[k, 3 * quarter : 4 * quarter, column] = mid_imag[quarter : 2 * quarter].astype(bf16)


def scale_of(part):
    return lax.rsqrt(jnp.sum(part) + 1e-06)


def statistics(k, first, fresh, scales, mids, last_ref, stat_ref):
    quarter = last_ref.shape[1] // 2
    half = 2 * quarter
    columns = pl.ds(pl.multiple_of(first * quarter, quarter), len(scales) * quarter)
    even = dot(last_ref[0], mids[k, :half, columns])
    odd = dot(last_ref[1], mids[k, half:, columns])
    for rows, sign in ((slice(0, half), 1), (slice(half, half + quarter), -1)):
        top = add = square = None
        for n, scale in enumerate(scales):
            e = even[: rows.stop - rows.start, n * quarter : (n + 1) * quarter]
            o = odd[: rows.stop - rows.start, n * quarter : (n + 1) * quarter]
            score = (e + o if sign > 0 else e - o) * scale
            top = score if n == 0 else jnp.maximum(top, score)
            add = score if n == 0 else add + score
            square = score * score if n == 0 else square + score * score
        if not fresh:
            top = jnp.maximum(stat_ref[0, rows], top)
            add = stat_ref[1, rows] + add
            square = stat_ref[2, rows] + square
        stat_ref[0, rows] = top
        stat_ref[1, rows] = add
        stat_ref[2, rows] = square


def finish(stats, searched):
    peak, add, squares = stats
    mean = add / searched
    variance = squares / searched - mean * mean
    return peak, (peak - mean) * lax.rsqrt(variance + 1e-06)


def flip(index, bits):
    at = 1
    while at <= bits:
        if bits & at:
            index = index + at * (1 - 2 * lax.rem(index // at, 2))
        at *= 2
    return index


def flip_by(index, bits, count):
    flipped, at = 0, 1
    while at < count:
        one, other = lax.rem(index // at, 2), lax.rem(bits // at, 2)
        flipped = flipped + at * (one + other - 2 * one * other)
        at *= 2
    return flipped


def search_kernel(
    n_tile, n_orient, valid,
    ids_hbm, off_hbm, x_hbm, lib_hbm, first_hbm, cos_hbm, sin_hbm, small_hbm, table_hbm, back_hbm,
    last_hbm, out_ref,
    ids_ref, off_ref, x_ref, lib_ref, first_ref, cos_ref, sin_ref, small_ref, table_ref, back_ref, last_ref,
    real_ref, imag_ref, halves_ref, sum_out, sum_in, total_ref, picks, parts, held, seen_real,
    seen_imag, seen_energy, gain_ref, base_ref, power_ref, part_ref, mids, stat_ref, share_out,
    share_in,
    local_sem, pick_send, pick_recv, spread_send, spread_recv,
    share_send, share_recv, sum_send, sum_recv, done_send, done_recv,
    out_send, out_recv,
):
    tile = lax.axis_index("tile")
    orient = lax.axis_index("orient")
    core = lax.rem(orient, 2)
    chip = orient // 2
    n_chip = n_orient // 2
    steps, size = picks.shape[0], picks.shape[1]
    slots = lib_ref.shape[0]
    tile_count, rows, length = real_ref.shape
    half, quarter = length // 2, length // 4
    partner = (tile, chip * 2 + 1 - core)
    tiles = [(flip(tile, k), orient) for k in range(1, n_tile)]
    chips = [(tile, flip(chip, k) * 2 + core) for k in range(1, n_chip)]

    def local(at, src, dst):
        copy = pltpu.make_async_copy(src, dst, local_sem.at[at])
        copy.start()
        return copy

    loads = dict(
        ids=local(9, ids_hbm, ids_ref),
        off=local(10, off_hbm, off_ref),
        lib=local(0, lib_hbm, lib_ref),
        x=local(1, x_hbm, x_ref),
        first=local(2, first_hbm, first_ref),
        cos=local(3, cos_hbm, cos_ref),
        sin=local(4, sin_hbm, sin_ref),
    )
    barrier = pltpu.get_barrier_semaphore()
    for device in [partner] + tiles + chips:
        pl.semaphore_signal(barrier, inc=1, device_id=device, device_id_type=MESH)

    def send(src, dst, send_sem, recv_sem, device):
        copy = pltpu.make_async_remote_copy(
            src_ref=src, dst_ref=dst, send_sem=send_sem, recv_sem=recv_sem,
            device_id=device, device_id_type=MESH,
        )
        copy.start()
        return copy

    loads["ids"].wait()
    loads["lib"].wait()
    for step in range(steps):
        chosen = ids_ref[0, step]
        owner = chosen // slots
        picked = lib_ref[chosen - owner * slots, 0]
        keep = jnp.where(owner == tile, 1.0, 0.0).astype(f32)
        picks[step] = jnp.where(keep > 0.0, picked.astype(f32), 0.0).astype(bf16)
    pl.semaphore_wait(barrier, 1 + len(tiles) + len(chips))
    pick_copies = [
        send(picks.at[step], parts.at[step, k], pick_send.at[step, k], pick_recv.at[step, k], device)
        for step in range(steps)
        for k, device in enumerate(tiles)
    ]
    loads["x"].wait()
    loads["first"].wait()
    for which in range(tile_count):
        halves_ref[which] = dot(first_ref[...], x_ref[which]).astype(bf16)

    loads["cos"].wait()
    loads["sin"].wait()
    loads.update(
        small=local(5, small_hbm, small_ref),
        table=local(6, table_hbm, table_ref),
        back=local(7, back_hbm, back_ref),
        last=local(8, last_hbm, last_ref),
    )

    def spectrum(side):
        columns = pl.ds(pl.multiple_of(side * half, half), half)
        cosine, sine = cos_ref[:, columns], sin_ref[:, columns]
        power = None
        for which in range(tile_count):
            half_real, half_imag = halves_ref[which, :rows], halves_ref[which, rows:]
            spec_real = dot(half_real, cosine) + dot(half_imag, sine)
            spec_imag = dot(half_imag, cosine) - dot(half_real, sine)
            real_ref[which, :, columns] = spec_real
            imag_ref[which, :, columns] = spec_imag
            share = spec_real * spec_real + spec_imag * spec_imag
            power = share if power is None else power + share
        return power

    total_ref[core] = spectrum(core)
    levels = sum_in.shape[0]
    cut = (rows // 32) * 16
    pieces = [pl.ds(0, cut), pl.ds(cut, rows - cut)]
    sums = {}

    def sum_step(s, piece):
        up, down = flip(tile, 1 << s), flip(tile, 1 << (levels - 1 - s))
        device = (up * (1 - core) + down * core, orient)
        at = s, pieces[piece]
        sum_out[at] = total_ref[core, pieces[piece]].astype(bf16)
        sems = sum_send.at[s, piece], sum_recv.at[s, piece]
        sums[s, piece] = send(sum_out.at[at], sum_in.at[at], *sems, device)

    def sum_wait(s, piece):
        sums[s, piece].wait()
        at = core, pieces[piece]
        total_ref[at] = total_ref[at] + sum_in[s, pieces[piece]].astype(f32)

    for piece in range(2):
        sum_step(0, piece)
    spectrum(1 - core)
    spread_copies = []
    for step in range(steps):
        template = picks[step].astype(f32)
        for k in range(len(tiles)):
            pick_copies[step * len(tiles) + k].wait()
            template = template + parts[step, k].astype(f32)
        held[chip, step] = template.astype(bf16)
        own = held.at[chip, step]
        spread_copies.append([
            send(own, own, spread_send.at[step, k], spread_recv.at[step, k], device)
            for k, device in enumerate(chips)
        ])
    loads["off"].wait()
    for which in range(tile_count):
        tilt = (off_ref[which, 0] - off_ref[which, 1]).astype(f32)
        tile_contrast(
            tilt, real_ref.at[which], imag_ref.at[which], seen_real.at[which],
            seen_imag.at[which], seen_energy.at[which],
        )

    batch = min(n_chip, 4)

    def spectra(place, at):
        images = held[place]
        images = jnp.concatenate([images[s] for s in range(steps)], axis=1)
        template_spectra(
            images, small_ref, table_ref, seen_real, seen_imag, seen_energy, base_ref, power_ref,
            lambda which, n: (which * batch + at) * steps + n,
        )

    def early(k):
        if n_chip == batch:
            spectra(flip(chip, k), flip(chip, k))

    loads["small"].wait()
    loads["table"].wait()
    for s in range(1, levels):
        for piece in range(2):
            sum_wait(s - 1, piece)
            sum_step(s, piece)
            if s == 1 and piece == 0:
                early(0)

    def arrive(k):
        for step in range(steps):
            spread_copies[step][k - 1].wait()
        early(k)

    near = (n_chip + 1) // 2
    for k in range(1, near):
        arrive(k)
    done_copies = []
    for piece in range(2):
        sum_wait(levels - 1, piece)
        mine = total_ref.at[core, pieces[piece]]
        done_copies.append(send(mine, mine, done_send.at[piece], done_recv.at[piece], partner))
    for k in range(near, n_chip):
        arrive(k)
    loads["back"].wait()
    loads["last"].wait()
    for copy in done_copies:
        copy.wait()
    tile_gains(n_tile * tile_count, total_ref, gain_ref)

    def search(begin, end):
        def visit(k, carry):
            place = flip_by(chip, k, batch) if n_chip == batch else k
            for which in range(2):
                for step in range(steps):
                    t = (which * batch + place) * steps + step
                    column = pl.ds(pl.multiple_of(t * quarter, quarter), quarter)
                    energy(t, power_ref, gain_ref, part_ref)
                    half_back(t, column, base_ref, back_ref, gain_ref, mids)
            return carry

        lax.fori_loop(begin, end, visit, 0)

    own = batch * steps
    rounds = n_chip // batch
    blocks = valid // quarter
    shares, out_copies = [], []
    for turn in range(rounds):
        if n_chip != batch:
            def fill(i, carry):
                spectra(turn * batch + i, i)
                return carry

            lax.fori_loop(0, batch, fill, 0)
        search(0, batch)
        for mine in range(2):
            which = core if mine else 1 - core
            scales = [scale_of(part_ref[which * own + n]) for n in range(own)]
            for k in range(blocks):
                stats = stat_ref.at[mine, k]
                for n in range(0, own, 2):
                    fresh = turn == 0 and n == 0
                    statistics(k, which * own + n, fresh, scales[n : n + 2], mids, last_ref, stats)
                if turn < rounds - 1:
                    continue
                if not mine:
                    share_out[k] = stats[...].astype(bf16)
                    sems = share_send.at[k], share_recv.at[k]
                    shares.append(send(share_out.at[k], share_in.at[k], *sems, partner))
                    continue
                shares[k].wait()
                other = share_in[k].astype(f32)
                peak = jnp.maximum(stats[0], other[0])
                joined = peak, stats[1] + other[1], stats[2] + other[2]
                found = finish(joined, 2 * rounds * own)
                columns = slice(k * quarter, (k + 1) * quarter)
                for kind in range(2):
                    out_ref[kind, core, :, columns] = found[kind].astype(bf16)
                    block = out_ref.at[kind, core, :, columns]
                    sems = out_send.at[k, kind], out_recv.at[k, kind]
                    out_copies.append(send(block, block, *sems, partner))
    for copy in out_copies:
        copy.wait()


def body(n_tile, n_orient, micrograph_tiles, tile_offsets, library, orient_ids):
    tile_count, length = micrograph_tiles.shape[:2]
    slots, _, size, _ = library.shape
    steps = orient_ids.shape[1]
    n_chip = n_orient // 2
    assert tile_count == 2 and n_orient % 2 == 0 and n_tile & (n_tile - 1) == 0 and n_chip & (n_chip - 1) == 0
    assert n_chip % min(n_chip, 4) == 0 and steps == 2
    half, quarter = length // 2, length // 4
    assert size == quarter and VALID % quarter == 0
    t = tables(length, size, VALID)
    rows = t["first"].shape[0] // 2
    names = ("first", "cos", "sin", "small", "base", "back", "last")
    count = tile_count * min(n_chip, 4) * steps
    levels = (n_tile - 1).bit_length()
    blocks = VALID // quarter
    shape = jax.ShapeDtypeStruct
    vmem, dma = pltpu.VMEM, pltpu.SemaphoreType.DMA
    operands = orient_ids, tile_offsets, micrograph_tiles, library, *[t[name] for name in names]
    both = pl.pallas_call(
        functools.partial(search_kernel, n_tile, n_orient, VALID),
        out_shape=shape((2, 2, VALID, VALID), bf16),
        in_specs=[HBM] * 11,
        out_specs=VMEM,
        scratch_shapes=[
            pltpu.SMEM(orient_ids.shape, jnp.int32),
            pltpu.SMEM(tile_offsets.shape, jnp.int32),
            vmem(micrograph_tiles.shape, bf16),
            vmem(library.shape, bf16),
            *[vmem(t[name].shape, bf16) for name in names],
            *[vmem((tile_count, rows, length), f32)] * 2,
            vmem((tile_count, 2 * rows, length), bf16),
            *[vmem((levels, rows, half), bf16)] * 2,
            vmem((2, rows, half), f32),
            vmem((steps, size, size), bf16),
            vmem((steps, n_tile - 1, size, size), bf16),
            vmem((n_chip, steps, size, size), bf16),
            *[vmem((tile_count, rows, length), bf16)] * 3,
            vmem((rows, length), bf16),
            vmem((count, rows, 2 * length), bf16),
            vmem((count, rows, length), bf16),
            vmem((count, 8, quarter), f32),
            vmem((blocks, length, count * quarter), bf16),
            vmem((2, blocks, 3, VALID, quarter), f32),
            *[vmem((blocks, 3, VALID, quarter), bf16)] * 2,
            dma((11,)),
            *[dma((steps, n_tile - 1))] * 2,
            *[dma((steps, n_chip - 1))] * 2,
            *[dma((blocks,))] * 2,
            *[dma((levels, 2))] * 2,
            *[dma((2,))] * 2,
            *[dma((blocks, 2))] * 2,
        ],
        compiler_params=pltpu.CompilerParams(
            collective_id=0, has_side_effects=True, vmem_limit_bytes=GRANT
        ),
    )(*[pltpu.with_memory_space_constraint(jnp.asarray(v), pltpu.HBM) for v in operands])
    return (both[0].astype(f32), both[1].astype(f32))


def solution(mesh):
    placed = (
        P("tile", None, None),
        P("tile", None),
        P("tile", "orient", None, None),
        P("orient", None),
    )
    return jax.shard_map(
        functools.partial(body, mesh.shape["tile"], mesh.shape["orient"]),
        mesh=mesh,
        in_specs=placed,
        out_specs=(P("tile", None, None), P("tile", None, None)),
        check_vma=False,
    )
```

```python
import functools
import math

import jax
import jax.numpy as jnp
import numpy as np
from jax import lax
from jax.experimental import pallas as pl
from jax.experimental.pallas import tpu as pltpu
from jax.sharding import PartitionSpec as P

VALID = 384
AMPLITUDE = 0.07
DEFOCUS_BASE = 100.0
DEFOCUS_TILT = 0.002
FLOOR_SHARE = 0.25
f32, bf16 = jnp.float32, jnp.bfloat16
MESH = pl.DeviceIdType.MESH
VMEM = pl.BlockSpec(memory_space=pltpu.VMEM)
HBM = pl.BlockSpec(memory_space=pltpu.HBM)
GRANT = 46 * 1024 * 1024


def tables(length, size, valid):
    half, quarter = length // 2, length // 4
    rows = -(-(half + 1) // 16) * 16
    b_index = np.concatenate([np.arange(0, half, 2), np.arange(1, half, 2), [half]])
    a_index = np.concatenate([np.arange(r, length, 4) for r in range(4)])
    j_index = np.arange(length)

    def wave(function, left, right):
        return function((left[:, None] * right[None, :]) % length * (2.0 * np.pi / length))

    first = np.zeros((2, rows, length))
    first[0, : half + 1] = wave(np.cos, b_index, j_index)
    first[1, : half + 1] = -wave(np.sin, b_index, j_index)
    cosine = wave(np.cos, j_index, a_index)
    sine = wave(np.sin, j_index, a_index)
    base, back = [], []
    for r in range(4):
        columns = slice(r * quarter, (r + 1) * quarter)
        c, s = cosine[:size, columns], sine[:size, columns]
        base.append((np.concatenate([c, s]), np.concatenate([-s, c])))
        c = wave(np.cos, a_index[columns], j_index[:quarter])
        s = wave(np.sin, a_index[columns], j_index[:quarter])
        back.append(np.block([[c, s], [-s, c]]))
    last = []
    for parity in range(2):
        b_part = b_index[parity * quarter : (parity + 1) * quarter]
        count = np.where(b_part == 0, 1.0, 2.0)
        c = wave(np.cos, j_index[:half], b_part) * count / length
        s = -wave(np.sin, j_index[:half], b_part) * count / length
        if parity == 0:
            s[:, 0] = np.cos(np.pi * j_index[:half]) / length
        last.append(np.concatenate([c, s], axis=1))

    def narrow(value):
        return np.asarray(value, np.float32).astype(jnp.bfloat16)

    first = first.reshape(2 * rows, length)
    return dict(
        first=narrow(first),
        small=narrow(np.ascontiguousarray(first[:, :size])),
        cos=narrow(cosine),
        sin=narrow(sine),
        base=narrow(np.concatenate([base[2 * p + q][w] for p in range(2) for w in range(2) for q in range(2)], axis=1)),
        back=narrow(np.stack(back)),
        last=narrow(np.stack(last)),
    )


def dot(left, right):
    return jnp.dot(left, right, preferred_element_type=jnp.float32)


def sine_of_turns(turns):
    part = turns - jnp.floor(turns + 0.5)
    mirrored = jnp.where(part > 0.0, 0.5, -0.5) - part
    part = jnp.where(jnp.abs(part) > 0.25, mirrored, part)
    angle = part * (2.0 * math.pi)
    square = angle * angle
    poly = -1.0 / 39916800.0
    for term in (1.0 / 362880.0, -1.0 / 5040.0, 1.0 / 120.0, -1.0 / 6.0, 1.0):
        poly = poly * square + term
    return angle * poly


def row_index(rows, half):
    row = lax.broadcasted_iota(jnp.int32, (rows, 1), 0)
    quarter = half // 2
    return row, jnp.where(row < quarter, 2 * row, jnp.where(row < half, 2 * row - half + 1, row))


def row_weight(rows, half):
    row, b_index = row_index(rows, half)
    single = (b_index == 0) | (row == half)
    return jnp.where(row > half, 0.0, jnp.where(single, 1.0, 2.0)).astype(f32)


def tile_contrast(tilt, real_ref, imag_ref, seen_real, seen_imag, seen_energy):
    rows, length = real_ref.shape
    half, quarter = length // 2, length // 4
    row, b_index = row_index(rows, half)
    b_index = jnp.where(row > half, 0, b_index).astype(f32) / length
    lane = lax.broadcasted_iota(jnp.int32, (1, length), 1)
    a_index = 4 * lax.rem(lane, quarter) + lane // quarter
    a_index = jnp.where(a_index < half, a_index, a_index - length).astype(f32) / length
    s2 = a_index * a_index + b_index * b_index
    defocus = DEFOCUS_BASE + DEFOCUS_TILT * tilt
    shift = math.asin(AMPLITUDE) / (2.0 * math.pi)
    contrast = -sine_of_turns(s2 * (0.5 * defocus) + shift)
    contrast = jnp.where(s2 > 0.0, contrast, 0.0)
    seen_real[...] = (real_ref[...] * contrast).astype(bf16)
    seen_imag[...] = (imag_ref[...] * contrast).astype(bf16)
    seen_energy[...] = (contrast * contrast * (row_weight(rows, half) / (length * length))).astype(bf16)


def template_spectra(
    images, small_ref, table_ref, seen_real, seen_imag, seen_energy, base_ref, power_ref, place
):
    rows = small_ref.shape[0] // 2
    size = images.shape[0]
    half = table_ref.shape[1] // 4
    halves = dot(small_ref[...], images).astype(bf16)
    for n in range(images.shape[1] // size):
        columns = slice(n * size, (n + 1) * size)
        joined = jnp.concatenate([halves[:rows, columns], halves[rows:, columns]], axis=1)
        for side in range(2):
            at = 2 * side * half
            columns = slice(side * half, (side + 1) * half)
            real = dot(joined, table_ref[:, at : at + half]).astype(bf16)
            imag = dot(joined, table_ref[:, at + half : at + 2 * half]).astype(bf16)
            power = real * real + imag * imag
            for which in range(seen_real.shape[0]):
                slot = place(which, n)
                left, right = seen_real[which, :, columns], seen_imag[which, :, columns]
                base_ref[slot, :, at : at + half] = left * real + right * imag
                base_ref[slot, :, at + half : at + 2 * half] = right * real - left * imag
                power_ref[slot, :, columns] = power * seen_energy[which, :, columns]


def tile_gains(tiles, total_ref, gain_ref):
    rows, length = gain_ref.shape
    half = length // 2
    weight = row_weight(rows, half)
    mean = (jnp.sum(total_ref[0] * weight) + jnp.sum(total_ref[1] * weight)) / tiles
    floor = FLOOR_SHARE * (mean / (length * length))
    for side in range(2):
        columns = slice(side * half, (side + 1) * half)
        gain_ref[:, columns] = (1.0 / jnp.maximum(total_ref[side] / tiles, floor)).astype(bf16)


def energy(t, power_ref, gain_ref, part_ref):
    rows, length = gain_ref.shape
    share = power_ref[t] * gain_ref[...]
    share = share[:, : length // 2] + share[:, length // 2 :]
    total = None
    for row in range(0, rows, 16):
        piece = share[row : row + 8] + share[row + 8 : row + 16]
        piece = piece.astype(f32)
        total = piece if total is None else total + piece
    part_ref[t] = total[:, : length // 4] + total[:, length // 4 :]


def half_back(t, column, base_ref, back_ref, gain_ref, mids):
    rows, length = gain_ref.shape
    quarter = length // 4
    half = 2 * quarter
    found = []
    for side in range(2):
        columns = slice(side * half, (side + 1) * half)
        at = 2 * side * half
        gain = gain_ref[:, columns]
        prod_real = base_ref[t, :, at : at + half] * gain
        prod_imag = base_ref[t, :, at + half : at + 2 * half] * gain
        for q in range(2):
            part = slice(q * quarter, (q + 1) * quarter)
            joined = jnp.concatenate([prod_real[:, part], prod_imag[:, part]], axis=1)
            found.append(dot(joined, back_ref[2 * side + q]))
    plus02, minus02 = found[0] + found[2], found[0] - found[2]
    plus13, minus13 = found[1] + found[3], found[1] - found[3]
    real, imag = slice(0, quarter), slice(quarter, 2 * quarter)
    out = (
        (plus02[:, real] + plus13[:, real], plus02[:, imag] + plus13[:, imag]),
        (minus02[:, real] - minus13[:, imag], minus02[:, imag] + minus13[:, real]),
        (plus02[:, real] - plus13[:, real], plus02[:, imag] - plus13[:, imag]),
    )
    row = lax.broadcasted_iota(jnp.int32, (quarter, quarter), 0)
    for k, (mid_real, mid_imag) in enumerate(out):
        top = jnp.where(row == 0, mid_real[2 * quarter : 2 * quarter + 1], mid_imag[:quarter])
        mids[k, 0:quarter, column] = mid_real[:quarter].astype(bf16)
        mids[k, quarter : 2 * quarter, column] = top.astype(bf16)
        mids[k, 2 * quarter : 3 * quarter, column] = mid_real[quarter : 2 * quarter].astype(bf16)
        mids[k, 3 * quarter : 4 * quarter, column] = mid_imag[quarter : 2 * quarter].astype(bf16)


def scale_of(part):
    return lax.rsqrt(jnp.sum(part) + 1e-06)


def statistics(k, first, fresh, scales, mids, last_ref, stat_ref):
    quarter = last_ref.shape[1] // 2
    half = 2 * quarter
    columns = pl.ds(pl.multiple_of(first * quarter, quarter), len(scales) * quarter)
    even = dot(last_ref[0], mids[k, :half, columns])
    odd = dot(last_ref[1], mids[k, half:, columns])
    for rows, sign in ((slice(0, half), 1), (slice(half, half + quarter), -1)):
        top = add = square = None
        for n, scale in enumerate(scales):
            e = even[: rows.stop - rows.start, n * quarter : (n + 1) * quarter]
            o = odd[: rows.stop - rows.start, n * quarter : (n + 1) * quarter]
            score = (e + o if sign > 0 else e - o) * scale
            top = score if n == 0 else jnp.maximum(top, score)
            add = score if n == 0 else add + score
            square = score * score if n == 0 else square + score * score
        if not fresh:
            top = jnp.maximum(stat_ref[0, rows], top)
            add = stat_ref[1, rows] + add
            square = stat_ref[2, rows] + square
        stat_ref[0, rows] = top
        stat_ref[1, rows] = add
        stat_ref[2, rows] = square


def finish(stats, searched):
    peak, add, squares = stats
    mean = add / searched
    variance = squares / searched - mean * mean
    return peak, (peak - mean) * lax.rsqrt(variance + 1e-06)


def flip(index, bits):
    at = 1
    while at <= bits:
        if bits & at:
            index = index + at * (1 - 2 * lax.rem(index // at, 2))
        at *= 2
    return index


def flip_by(index, bits, count):
    flipped, at = 0, 1
    while at < count:
        one, other = lax.rem(index // at, 2), lax.rem(bits // at, 2)
        flipped = flipped + at * (one + other - 2 * one * other)
        at *= 2
    return flipped


def search_kernel(
    n_tile, n_orient, valid,
    ids_hbm, off_hbm, x_hbm, lib_hbm, first_hbm, cos_hbm, sin_hbm, small_hbm, table_hbm, back_hbm,
    last_hbm, out_ref,
    ids_ref, off_ref, x_ref, lib_ref, first_ref, cos_ref, sin_ref, small_ref, table_ref, back_ref, last_ref,
    real_ref, imag_ref, halves_ref, sum_out, sum_in, total_ref, picks, parts, held, seen_real,
    seen_imag, seen_energy, gain_ref, base_ref, power_ref, part_ref, mids, stat_ref, share_out,
    share_in,
    local_sem, pick_send, pick_recv, spread_send, spread_recv,
    share_send, share_recv, sum_send, sum_recv, done_send, done_recv,
    out_send, out_recv,
):
    tile = lax.axis_index("tile")
    orient = lax.axis_index("orient")
    core = lax.rem(orient, 2)
    chip = orient // 2
    n_chip = n_orient // 2
    steps, size = picks.shape[0], picks.shape[1]
    slots = lib_ref.shape[0]
    tile_count, rows, length = real_ref.shape
    half, quarter = length // 2, length // 4
    partner = (tile, chip * 2 + 1 - core)
    tiles = [(flip(tile, k), orient) for k in range(1, n_tile)]
    chips = [(tile, flip(chip, k) * 2 + core) for k in range(1, n_chip)]

    def local(at, src, dst):
        copy = pltpu.make_async_copy(src, dst, local_sem.at[at])
        copy.start()
        return copy

    loads = dict(
        ids=local(9, ids_hbm, ids_ref),
        off=local(10, off_hbm, off_ref),
        lib=local(0, lib_hbm, lib_ref),
    )
    barrier = pltpu.get_barrier_semaphore()
    for device in [partner] + tiles + chips:
        pl.semaphore_signal(barrier, inc=1, device_id=device, device_id_type=MESH)
    loads.update(
        x=local(1, x_hbm, x_ref),
        first=local(2, first_hbm, first_ref),
        cos=local(3, cos_hbm, cos_ref),
        sin=local(4, sin_hbm, sin_ref),
    )
    def send(src, dst, send_sem, recv_sem, device):
        copy = pltpu.make_async_remote_copy(
            src_ref=src, dst_ref=dst, send_sem=send_sem, recv_sem=recv_sem,
            device_id=device, device_id_type=MESH,
        )
        copy.start()
        return copy

    loads["ids"].wait()
    loads["lib"].wait()
    for step in range(steps):
        chosen = ids_ref[0, step]
        owner = chosen // slots
        picked = lib_ref[chosen - owner * slots, 0]
        keep = jnp.where(owner == tile, 1.0, 0.0).astype(f32)
        picks[step] = jnp.where(keep > 0.0, picked.astype(f32), 0.0).astype(bf16)
    pl.semaphore_wait(barrier, 1 + len(tiles) + len(chips))
    pick_copies = [
        send(picks.at[step], parts.at[step, k], pick_send.at[step, k], pick_recv.at[step, k], device)
        for step in range(steps)
        for k, device in enumerate(tiles)
    ]
    loads["x"].wait()
    loads["first"].wait()
    for which in range(tile_count):
        halves_ref[which] = dot(first_ref[...], x_ref[which]).astype(bf16)

    loads["cos"].wait()
    loads["sin"].wait()
    loads.update(
        small=local(5, small_hbm, small_ref),
        table=local(6, table_hbm, table_ref),
        back=local(7, back_hbm, back_ref),
        last=local(8, last_hbm, last_ref),
    )

    def spectrum(side):
        columns = pl.ds(pl.multiple_of(side * half, half), half)
        cosine, sine = cos_ref[:, columns], sin_ref[:, columns]
        power = None
        for which in range(tile_count):
            half_real, half_imag = halves_ref[which, :rows], halves_ref[which, rows:]
            spec_real = dot(half_real, cosine) + dot(half_imag, sine)
            spec_imag = dot(half_imag, cosine) - dot(half_real, sine)
            real_ref[which, :, columns] = spec_real
            imag_ref[which, :, columns] = spec_imag
            share = spec_real * spec_real + spec_imag * spec_imag
            power = share if power is None else power + share
        return power

    total_ref[core] = spectrum(core)
    levels = sum_in.shape[0]
    cut = (rows // 32) * 16
    pieces = [pl.ds(0, cut), pl.ds(cut, rows - cut)]
    sums = {}

    def sum_step(s, piece):
        up, down = flip(tile, 1 << s), flip(tile, 1 << (levels - 1 - s))
        device = (up * (1 - core) + down * core, orient)
        at = s, pieces[piece]
        sum_out[at] = total_ref[core, pieces[piece]].astype(bf16)
        sems = sum_send.at[s, piece], sum_recv.at[s, piece]
        sums[s, piece] = send(sum_out.at[at], sum_in.at[at], *sems, device)

    def sum_wait(s, piece):
        sums[s, piece].wait()
        at = core, pieces[piece]
        total_ref[at] = total_ref[at] + sum_in[s, pieces[piece]].astype(f32)

    for piece in range(2):
        sum_step(0, piece)
    spectrum(1 - core)
    loads["off"].wait()
    for which in range(tile_count):
        tilt = (off_ref[which, 0] - off_ref[which, 1]).astype(f32)
        tile_contrast(
            tilt, real_ref.at[which], imag_ref.at[which], seen_real.at[which],
            seen_imag.at[which], seen_energy.at[which],
        )
    spread_copies = []
    for step in range(steps):
        template = picks[step].astype(f32)
        for k in range(len(tiles)):
            pick_copies[step * len(tiles) + k].wait()
            template = template + parts[step, k].astype(f32)
        held[chip, step] = template.astype(bf16)
        own = held.at[chip, step]
        spread_copies.append([
            send(own, own, spread_send.at[step, k], spread_recv.at[step, k], device)
            for k, device in enumerate(chips)
        ])
    batch = min(n_chip, 4)

    def spectra(place, at):
        images = held[place]
        images = jnp.concatenate([images[s] for s in range(steps)], axis=1)
        template_spectra(
            images, small_ref, table_ref, seen_real, seen_imag, seen_energy, base_ref, power_ref,
            lambda which, n: (which * batch + at) * steps + n,
        )

    def early(k):
        if n_chip == batch:
            spectra(flip(chip, k), flip(chip, k))

    loads["small"].wait()
    loads["table"].wait()
    early(0)
    for s in range(1, levels):
        for piece in range(2):
            sum_wait(s - 1, piece)
            sum_step(s, piece)

    def arrive(k):
        for step in range(steps):
            spread_copies[step][k - 1].wait()
        early(k)

    near = (n_chip + 1) // 2
    for k in range(1, near):
        arrive(k)
    done_copies = []
    for piece in range(2):
        sum_wait(levels - 1, piece)
        mine = total_ref.at[core, pieces[piece]]
        done_copies.append(send(mine, mine, done_send.at[piece], done_recv.at[piece], partner))
    for k in range(near, n_chip):
        arrive(k)
    loads["back"].wait()
    loads["last"].wait()
    for copy in done_copies:
        copy.wait()
    tile_gains(n_tile * tile_count, total_ref, gain_ref)

    def search(begin, end):
        def visit(k, carry):
            place = flip_by(chip, k, batch) if n_chip == batch else k
            for which in range(2):
                for step in range(steps):
                    t = (which * batch + place) * steps + step
                    column = pl.ds(pl.multiple_of(t * quarter, quarter), quarter)
                    energy(t, power_ref, gain_ref, part_ref)
                    half_back(t, column, base_ref, back_ref, gain_ref, mids)
            return carry

        lax.fori_loop(begin, end, visit, 0, unroll=2)

    own = batch * steps
    rounds = n_chip // batch
    blocks = valid // quarter
    shares, out_copies = [], []
    for turn in range(rounds):
        if n_chip != batch:
            def fill(i, carry):
                spectra(turn * batch + i, i)
                return carry

            lax.fori_loop(0, batch, fill, 0)
        search(0, batch)
        for mine in range(2):
            which = core if mine else 1 - core
            scales = [scale_of(part_ref[which * own + n]) for n in range(own)]
            for k in range(blocks):
                stats = stat_ref.at[mine, k]
                for n in range(0, own, 2):
                    fresh = turn == 0 and n == 0
                    statistics(k, which * own + n, fresh, scales[n : n + 2], mids, last_ref, stats)
                if turn < rounds - 1:
                    continue
                if not mine:
                    share_out[k] = stats[...].astype(bf16)
                    sems = share_send.at[k], share_recv.at[k]
                    shares.append(send(share_out.at[k], share_in.at[k], *sems, partner))
                    continue
                shares[k].wait()
                other = share_in[k].astype(f32)
                peak = jnp.maximum(stats[0], other[0])
                joined = peak, stats[1] + other[1], stats[2] + other[2]
                found = finish(joined, 2 * rounds * own)
                columns = slice(k * quarter, (k + 1) * quarter)
                for kind in range(2):
                    out_ref[kind, core, :, columns] = found[kind].astype(bf16)
                    block = out_ref.at[kind, core, :, columns]
                    sems = out_send.at[k, kind], out_recv.at[k, kind]
                    out_copies.append(send(block, block, *sems, partner))
    for copy in out_copies:
        copy.wait()


def body(n_tile, n_orient, micrograph_tiles, tile_offsets, library, orient_ids):
    tile_count, length = micrograph_tiles.shape[:2]
    slots, _, size, _ = library.shape
    steps = orient_ids.shape[1]
    n_chip = n_orient // 2
    assert tile_count == 2 and n_orient % 2 == 0 and n_tile & (n_tile - 1) == 0 and n_chip & (n_chip - 1) == 0
    assert n_chip % min(n_chip, 4) == 0 and steps == 2
    half, quarter = length // 2, length // 4
    assert size == quarter and VALID % quarter == 0
    t = tables(length, size, VALID)
    rows = t["first"].shape[0] // 2
    names = ("first", "cos", "sin", "small", "base", "back", "last")
    count = tile_count * min(n_chip, 4) * steps
    levels = (n_tile - 1).bit_length()
    blocks = VALID // quarter
    shape = jax.ShapeDtypeStruct
    vmem, dma = pltpu.VMEM, pltpu.SemaphoreType.DMA
    operands = orient_ids, tile_offsets, micrograph_tiles, library, *[t[name] for name in names]
    both = pl.pallas_call(
        functools.partial(search_kernel, n_tile, n_orient, VALID),
        out_shape=shape((2, 2, VALID, VALID), bf16),
        in_specs=[HBM] * 11,
        out_specs=VMEM,
        scratch_shapes=[
            pltpu.SMEM(orient_ids.shape, jnp.int32),
            pltpu.SMEM(tile_offsets.shape, jnp.int32),
            vmem(micrograph_tiles.shape, bf16),
            vmem(library.shape, bf16),
            *[vmem(t[name].shape, bf16) for name in names],
            *[vmem((tile_count, rows, length), f32)] * 2,
            vmem((tile_count, 2 * rows, length), bf16),
            *[vmem((levels, rows, half), bf16)] * 2,
            vmem((2, rows, half), f32),
            vmem((steps, size, size), bf16),
            vmem((steps, n_tile - 1, size, size), bf16),
            vmem((n_chip, steps, size, size), bf16),
            *[vmem((tile_count, rows, length), bf16)] * 3,
            vmem((rows, length), bf16),
            vmem((count, rows, 2 * length), bf16),
            vmem((count, rows, length), bf16),
            vmem((count, 8, quarter), f32),
            vmem((blocks, length, count * quarter), bf16),
            vmem((2, blocks, 3, VALID, quarter), f32),
            *[vmem((blocks, 3, VALID, quarter), bf16)] * 2,
            dma((11,)),
            *[dma((steps, n_tile - 1))] * 2,
            *[dma((steps, n_chip - 1))] * 2,
            *[dma((blocks,))] * 2,
            *[dma((levels, 2))] * 2,
            *[dma((2,))] * 2,
            *[dma((blocks, 2))] * 2,
        ],
        compiler_params=pltpu.CompilerParams(
            collective_id=0, has_side_effects=True, vmem_limit_bytes=GRANT
        ),
    )(*[pltpu.with_memory_space_constraint(jnp.asarray(v), pltpu.HBM) for v in operands])
    return (both[0].astype(f32), both[1].astype(f32))


def solution(mesh):
    placed = (
        P("tile", None, None),
        P("tile", None),
        P("tile", "orient", None, None),
        P("orient", None),
    )
    return jax.shard_map(
        functools.partial(body, mesh.shape["tile"], mesh.shape["orient"]),
        mesh=mesh,
        in_specs=placed,
        out_specs=(P("tile", None, None), P("tile", None, None)),
        check_vma=False,
    )
```

```python
import functools
import math

import jax
import jax.numpy as jnp
import numpy as np
from jax import lax
from jax.experimental import pallas as pl
from jax.experimental.pallas import tpu as pltpu
from jax.sharding import PartitionSpec as P

VALID = 384
AMPLITUDE = 0.07
DEFOCUS_BASE = 100.0
DEFOCUS_TILT = 0.002
FLOOR_SHARE = 0.25
f32, bf16 = jnp.float32, jnp.bfloat16
MESH = pl.DeviceIdType.MESH
VMEM = pl.BlockSpec(memory_space=pltpu.VMEM)
HBM = pl.BlockSpec(memory_space=pltpu.HBM)
GRANT = 46 * 1024 * 1024


def tables(length, size, valid):
    half, quarter = length // 2, length // 4
    rows = -(-(half + 1) // 16) * 16
    b_index = np.concatenate([np.arange(0, half, 2), np.arange(1, half, 2), [half]])
    a_index = np.concatenate([np.arange(r, length, 4) for r in range(4)])
    j_index = np.arange(length)

    def wave(function, left, right):
        return function((left[:, None] * right[None, :]) % length * (2.0 * np.pi / length))

    first = np.zeros((2, rows, length))
    first[0, : half + 1] = wave(np.cos, b_index, j_index)
    first[1, : half + 1] = -wave(np.sin, b_index, j_index)
    cosine = wave(np.cos, j_index, a_index)
    sine = wave(np.sin, j_index, a_index)
    base, back = [], []
    for r in range(4):
        columns = slice(r * quarter, (r + 1) * quarter)
        c, s = cosine[:size, columns], sine[:size, columns]
        base.append((np.concatenate([c, s]), np.concatenate([-s, c])))
        c = wave(np.cos, a_index[columns], j_index[:quarter])
        s = wave(np.sin, a_index[columns], j_index[:quarter])
        back.append(np.block([[c, s], [-s, c]]))
    last = []
    for parity in range(2):
        b_part = b_index[parity * quarter : (parity + 1) * quarter]
        count = np.where(b_part == 0, 1.0, 2.0)
        c = wave(np.cos, j_index[:half], b_part) * count / length
        s = -wave(np.sin, j_index[:half], b_part) * count / length
        if parity == 0:
            s[:, 0] = np.cos(np.pi * j_index[:half]) / length
        last.append(np.concatenate([c, s], axis=1))

    def narrow(value):
        return np.asarray(value, np.float32).astype(jnp.bfloat16)

    first = first.reshape(2 * rows, length)
    return dict(
        first=narrow(first),
        small=narrow(np.ascontiguousarray(first[:, :size])),
        cos=narrow(cosine),
        sin=narrow(sine),
        base=narrow(np.concatenate([base[2 * p + q][w] for p in range(2) for w in range(2) for q in range(2)], axis=1)),
        back=narrow(np.stack(back)),
        last=narrow(np.stack(last)),
    )


def dot(left, right):
    return jnp.dot(left, right, preferred_element_type=jnp.float32)


def sine_of_turns(turns):
    part = turns - jnp.floor(turns + 0.5)
    mirrored = jnp.where(part > 0.0, 0.5, -0.5) - part
    part = jnp.where(jnp.abs(part) > 0.25, mirrored, part)
    angle = part * (2.0 * math.pi)
    square = angle * angle
    poly = -1.0 / 39916800.0
    for term in (1.0 / 362880.0, -1.0 / 5040.0, 1.0 / 120.0, -1.0 / 6.0, 1.0):
        poly = poly * square + term
    return angle * poly


def row_index(rows, half):
    row = lax.broadcasted_iota(jnp.int32, (rows, 1), 0)
    quarter = half // 2
    return row, jnp.where(row < quarter, 2 * row, jnp.where(row < half, 2 * row - half + 1, row))


def row_weight(rows, half):
    row, b_index = row_index(rows, half)
    single = (b_index == 0) | (row == half)
    return jnp.where(row > half, 0.0, jnp.where(single, 1.0, 2.0)).astype(f32)


def tile_contrast(tilt, real_ref, imag_ref, seen_real, seen_imag, seen_energy):
    rows, length = real_ref.shape
    half, quarter = length // 2, length // 4
    row, b_index = row_index(rows, half)
    b_index = jnp.where(row > half, 0, b_index).astype(f32) / length
    lane = lax.broadcasted_iota(jnp.int32, (1, length), 1)
    a_index = 4 * lax.rem(lane, quarter) + lane // quarter
    a_index = jnp.where(a_index < half, a_index, a_index - length).astype(f32) / length
    s2 = a_index * a_index + b_index * b_index
    defocus = DEFOCUS_BASE + DEFOCUS_TILT * tilt
    shift = math.asin(AMPLITUDE) / (2.0 * math.pi)
    contrast = -sine_of_turns(s2 * (0.5 * defocus) + shift)
    contrast = jnp.where(s2 > 0.0, contrast, 0.0)
    seen_real[...] = (real_ref[...] * contrast).astype(bf16)
    seen_imag[...] = (imag_ref[...] * contrast).astype(bf16)
    seen_energy[...] = (contrast * contrast * (row_weight(rows, half) / (length * length))).astype(bf16)


def template_spectra(
    images, small_ref, table_ref, seen_real, seen_imag, seen_energy, base_ref, power_ref, place
):
    rows = small_ref.shape[0] // 2
    size = images.shape[0]
    half = table_ref.shape[1] // 4
    halves = dot(small_ref[...], images).astype(bf16)
    for n in range(images.shape[1] // size):
        columns = slice(n * size, (n + 1) * size)
        joined = jnp.concatenate([halves[:rows, columns], halves[rows:, columns]], axis=1)
        for side in range(2):
            at = 2 * side * half
            columns = slice(side * half, (side + 1) * half)
            real = dot(joined, table_ref[:, at : at + half]).astype(bf16)
            imag = dot(joined, table_ref[:, at + half : at + 2 * half]).astype(bf16)
            power = real * real + imag * imag
            for which in range(seen_real.shape[0]):
                slot = place(which, n)
                left, right = seen_real[which, :, columns], seen_imag[which, :, columns]
                base_ref[slot, :, at : at + half] = left * real + right * imag
                base_ref[slot, :, at + half : at + 2 * half] = right * real - left * imag
                power_ref[slot, :, columns] = power * seen_energy[which, :, columns]


def tile_gains(tiles, total_ref, gain_ref):
    rows, length = gain_ref.shape
    half = length // 2
    weight = row_weight(rows, half)
    mean = (jnp.sum(total_ref[0] * weight) + jnp.sum(total_ref[1] * weight)) / tiles
    floor = FLOOR_SHARE * (mean / (length * length))
    for side in range(2):
        columns = slice(side * half, (side + 1) * half)
        gain_ref[:, columns] = (1.0 / jnp.maximum(total_ref[side] / tiles, floor)).astype(bf16)


def energy(t, power_ref, gain_ref, part_ref):
    rows, length = gain_ref.shape
    share = power_ref[t] * gain_ref[...]
    share = share[:, : length // 2] + share[:, length // 2 :]
    total = None
    for row in range(0, rows, 16):
        piece = share[row : row + 8] + share[row + 8 : row + 16]
        piece = piece.astype(f32)
        total = piece if total is None else total + piece
    part_ref[t] = total[:, : length // 4] + total[:, length // 4 :]


def half_back(t, column, base_ref, back_ref, gain_ref, mids):
    rows, length = gain_ref.shape
    quarter = length // 4
    half = 2 * quarter
    found = []
    for side in range(2):
        columns = slice(side * half, (side + 1) * half)
        at = 2 * side * half
        gain = gain_ref[:, columns]
        prod_real = base_ref[t, :, at : at + half] * gain
        prod_imag = base_ref[t, :, at + half : at + 2 * half] * gain
        for q in range(2):
            part = slice(q * quarter, (q + 1) * quarter)
            joined = jnp.concatenate([prod_real[:, part], prod_imag[:, part]], axis=1)
            found.append(dot(joined, back_ref[2 * side + q]))
    plus02, minus02 = found[0] + found[2], found[0] - found[2]
    plus13, minus13 = found[1] + found[3], found[1] - found[3]
    real, imag = slice(0, quarter), slice(quarter, 2 * quarter)
    out = (
        (plus02[:, real] + plus13[:, real], plus02[:, imag] + plus13[:, imag]),
        (minus02[:, real] - minus13[:, imag], minus02[:, imag] + minus13[:, real]),
        (plus02[:, real] - plus13[:, real], plus02[:, imag] - plus13[:, imag]),
    )
    row = lax.broadcasted_iota(jnp.int32, (quarter, quarter), 0)
    for k, (mid_real, mid_imag) in enumerate(out):
        top = jnp.where(row == 0, mid_real[2 * quarter : 2 * quarter + 1], mid_imag[:quarter])
        mids[k, 0:quarter, column] = mid_real[:quarter].astype(bf16)
        mids[k, quarter : 2 * quarter, column] = top.astype(bf16)
        mids[k, 2 * quarter : 3 * quarter, column] = mid_real[quarter : 2 * quarter].astype(bf16)
        mids[k, 3 * quarter : 4 * quarter, column] = mid_imag[quarter : 2 * quarter].astype(bf16)


def scale_of(part):
    return lax.rsqrt(jnp.sum(part) + 1e-06)


def statistics(k, first, fresh, scales, mids, last_ref, stat_ref):
    quarter = last_ref.shape[1] // 2
    half = 2 * quarter
    columns = pl.ds(pl.multiple_of(first * quarter, quarter), len(scales) * quarter)
    even = dot(last_ref[0], mids[k, :half, columns])
    odd = dot(last_ref[1], mids[k, half:, columns])
    for rows, sign in ((slice(0, half), 1), (slice(half, half + quarter), -1)):
        top = add = square = None
        for n, scale in enumerate(scales):
            e = even[: rows.stop - rows.start, n * quarter : (n + 1) * quarter]
            o = odd[: rows.stop - rows.start, n * quarter : (n + 1) * quarter]
            score = (e + o if sign > 0 else e - o) * scale
            top = score if n == 0 else jnp.maximum(top, score)
            add = score if n == 0 else add + score
            square = score * score if n == 0 else square + score * score
        if not fresh:
            top = jnp.maximum(stat_ref[0, rows], top)
            add = stat_ref[1, rows] + add
            square = stat_ref[2, rows] + square
        stat_ref[0, rows] = top
        stat_ref[1, rows] = add
        stat_ref[2, rows] = square


def finish(stats, searched):
    peak, add, squares = stats
    mean = add / searched
    variance = squares / searched - mean * mean
    return peak, (peak - mean) * lax.rsqrt(variance + 1e-06)


def flip(index, bits):
    at = 1
    while at <= bits:
        if bits & at:
            index = index + at * (1 - 2 * lax.rem(index // at, 2))
        at *= 2
    return index


def flip_by(index, bits, count):
    flipped, at = 0, 1
    while at < count:
        one, other = lax.rem(index // at, 2), lax.rem(bits // at, 2)
        flipped = flipped + at * (one + other - 2 * one * other)
        at *= 2
    return flipped


def search_kernel(
    n_tile, n_orient, valid,
    ids_hbm, off_hbm, x_hbm, lib_hbm, first_hbm, cos_hbm, sin_hbm, small_hbm, table_hbm, back_hbm,
    last_hbm, out_ref,
    ids_ref, off_ref, x_ref, lib_ref, first_ref, cos_ref, sin_ref, small_ref, table_ref, back_ref, last_ref,
    real_ref, imag_ref, halves_ref, sum_out, sum_in, total_ref, picks, parts, held, seen_real,
    seen_imag, seen_energy, gain_ref, base_ref, power_ref, part_ref, mids, stat_ref, share_out,
    share_in,
    local_sem, pick_send, pick_recv, spread_send, spread_recv,
    share_send, share_recv, sum_send, sum_recv, done_send, done_recv,
    out_send, out_recv,
):
    tile = lax.axis_index("tile")
    orient = lax.axis_index("orient")
    core = lax.rem(orient, 2)
    chip = orient // 2
    n_chip = n_orient // 2
    steps, size = picks.shape[0], picks.shape[1]
    slots = lib_ref.shape[0]
    tile_count, rows, length = real_ref.shape
    half, quarter = length // 2, length // 4
    partner = (tile, chip * 2 + 1 - core)
    tiles = [(flip(tile, k), orient) for k in range(1, n_tile)]
    chips = [(tile, flip(chip, k) * 2 + core) for k in range(1, n_chip)]

    def local(at, src, dst):
        copy = pltpu.make_async_copy(src, dst, local_sem.at[at])
        copy.start()
        return copy

    loads = dict(
        ids=local(9, ids_hbm, ids_ref),
        off=local(10, off_hbm, off_ref),
        lib=local(0, lib_hbm, lib_ref),
    )
    barrier = pltpu.get_barrier_semaphore()
    for device in [partner] + tiles + chips:
        pl.semaphore_signal(barrier, inc=1, device_id=device, device_id_type=MESH)
    loads.update(
        x=local(1, x_hbm, x_ref),
        first=local(2, first_hbm, first_ref),
        cos=local(3, cos_hbm, cos_ref),
        sin=local(4, sin_hbm, sin_ref),
    )
    def send(src, dst, send_sem, recv_sem, device):
        copy = pltpu.make_async_remote_copy(
            src_ref=src, dst_ref=dst, send_sem=send_sem, recv_sem=recv_sem,
            device_id=device, device_id_type=MESH,
        )
        copy.start()
        return copy

    loads["ids"].wait()
    loads["lib"].wait()
    for step in range(steps):
        chosen = ids_ref[0, step]
        owner = chosen // slots
        picked = lib_ref[chosen - owner * slots, 0]
        keep = jnp.where(owner == tile, 1.0, 0.0).astype(f32)
        picks[step] = jnp.where(keep > 0.0, picked.astype(f32), 0.0).astype(bf16)
    pl.semaphore_wait(barrier, 1 + len(tiles) + len(chips))
    pick_copies = [
        send(picks.at[step], parts.at[step, k], pick_send.at[step, k], pick_recv.at[step, k], device)
        for step in range(steps)
        for k, device in enumerate(tiles)
    ]
    loads["x"].wait()
    loads["first"].wait()
    for which in range(tile_count):
        halves_ref[which] = dot(first_ref[...], x_ref[which]).astype(bf16)

    loads["cos"].wait()
    loads["sin"].wait()
    loads.update(
        small=local(5, small_hbm, small_ref),
        table=local(6, table_hbm, table_ref),
        back=local(7, back_hbm, back_ref),
        last=local(8, last_hbm, last_ref),
    )

    def spectrum(side):
        columns = pl.ds(pl.multiple_of(side * half, half), half)
        cosine, sine = cos_ref[:, columns], sin_ref[:, columns]
        power = None
        for which in range(tile_count):
            half_real, half_imag = halves_ref[which, :rows], halves_ref[which, rows:]
            spec_real = dot(half_real, cosine) + dot(half_imag, sine)
            spec_imag = dot(half_imag, cosine) - dot(half_real, sine)
            real_ref[which, :, columns] = spec_real
            imag_ref[which, :, columns] = spec_imag
            share = spec_real * spec_real + spec_imag * spec_imag
            power = share if power is None else power + share
        return power

    total_ref[core] = spectrum(core)
    levels = sum_in.shape[0]
    cut = (rows // 32) * 16
    pieces = [pl.ds(0, cut), pl.ds(cut, rows - cut)]
    sums = {}

    def sum_step(s, piece):
        up, down = flip(tile, 1 << s), flip(tile, 1 << (levels - 1 - s))
        device = (up * (1 - core) + down * core, orient)
        at = s, pieces[piece]
        sum_out[at] = total_ref[core, pieces[piece]].astype(bf16)
        sems = sum_send.at[s, piece], sum_recv.at[s, piece]
        sums[s, piece] = send(sum_out.at[at], sum_in.at[at], *sems, device)

    def sum_wait(s, piece):
        sums[s, piece].wait()
        at = core, pieces[piece]
        total_ref[at] = total_ref[at] + sum_in[s, pieces[piece]].astype(f32)

    for piece in range(2):
        sum_step(0, piece)
    spectrum(1 - core)
    loads["off"].wait()
    for which in range(tile_count):
        tilt = (off_ref[which, 0] - off_ref[which, 1]).astype(f32)
        tile_contrast(
            tilt, real_ref.at[which], imag_ref.at[which], seen_real.at[which],
            seen_imag.at[which], seen_energy.at[which],
        )
    spread_copies = []
    for step in range(steps):
        template = picks[step].astype(f32)
        for k in range(len(tiles)):
            pick_copies[step * len(tiles) + k].wait()
            template = template + parts[step, k].astype(f32)
        held[chip, step] = template.astype(bf16)
        own = held.at[chip, step]
        spread_copies.append([
            send(own, own, spread_send.at[step, k], spread_recv.at[step, k], device)
            for k, device in enumerate(chips)
        ])
    batch = min(n_chip, 4)

    def spectra(place, at):
        images = held[place]
        images = jnp.concatenate([images[s] for s in range(steps)], axis=1)
        template_spectra(
            images, small_ref, table_ref, seen_real, seen_imag, seen_energy, base_ref, power_ref,
            lambda which, n: (which * batch + at) * steps + n,
        )

    def early(k):
        if n_chip == batch:
            spectra(flip(chip, k), flip(chip, k))

    loads["small"].wait()
    loads["table"].wait()
    early(0)
    for s in range(1, levels):
        for piece in range(2):
            sum_wait(s - 1, piece)
            sum_step(s, piece)

    def arrive(k):
        for step in range(steps):
            spread_copies[step][k - 1].wait()
        early(k)

    near = (n_chip + 1) // 2
    for k in range(1, near):
        arrive(k)
    done_copies = []
    for piece in range(2):
        sum_wait(levels - 1, piece)
        mine = total_ref.at[core, pieces[piece]]
        done_copies.append(send(mine, mine, done_send.at[piece], done_recv.at[piece], partner))
    for k in range(near, n_chip):
        arrive(k)
    loads["back"].wait()
    loads["last"].wait()
    for copy in done_copies:
        copy.wait()
    tile_gains(n_tile * tile_count, total_ref, gain_ref)

    def search(begin, end):
        def visit(k, carry):
            place = flip_by(chip, k, batch) if n_chip == batch else k
            for which in range(2):
                for step in range(steps):
                    t = (which * batch + place) * steps + step
                    column = pl.ds(pl.multiple_of(t * quarter, quarter), quarter)
                    energy(t, power_ref, gain_ref, part_ref)
                    half_back(t, column, base_ref, back_ref, gain_ref, mids)
            return carry

        lax.fori_loop(begin, end, visit, 0, unroll=batch if n_chip == batch else 1)

    own = batch * steps
    rounds = n_chip // batch
    blocks = valid // quarter
    shares, out_copies = [], []
    for turn in range(rounds):
        if n_chip != batch:
            def fill(i, carry):
                spectra(turn * batch + i, i)
                return carry

            lax.fori_loop(0, batch, fill, 0)
        search(0, batch)
        for mine in range(2):
            which = core if mine else 1 - core
            scales = [scale_of(part_ref[which * own + n]) for n in range(own)]
            for k in range(blocks):
                stats = stat_ref.at[mine, k]
                for n in range(0, own, 2):
                    fresh = turn == 0 and n == 0
                    statistics(k, which * own + n, fresh, scales[n : n + 2], mids, last_ref, stats)
                if turn < rounds - 1:
                    continue
                if not mine:
                    share_out[k] = stats[...].astype(bf16)
                    sems = share_send.at[k], share_recv.at[k]
                    shares.append(send(share_out.at[k], share_in.at[k], *sems, partner))
                    continue
                shares[k].wait()
                other = share_in[k].astype(f32)
                peak = jnp.maximum(stats[0], other[0])
                joined = peak, stats[1] + other[1], stats[2] + other[2]
                found = finish(joined, 2 * rounds * own)
                columns = slice(k * quarter, (k + 1) * quarter)
                for kind in range(2):
                    out_ref[kind, core, :, columns] = found[kind].astype(bf16)
                    block = out_ref.at[kind, core, :, columns]
                    sems = out_send.at[k, kind], out_recv.at[k, kind]
                    out_copies.append(send(block, block, *sems, partner))
    for copy in out_copies:
        copy.wait()


def body(n_tile, n_orient, micrograph_tiles, tile_offsets, library, orient_ids):
    tile_count, length = micrograph_tiles.shape[:2]
    slots, _, size, _ = library.shape
    steps = orient_ids.shape[1]
    n_chip = n_orient // 2
    assert tile_count == 2 and n_orient % 2 == 0 and n_tile & (n_tile - 1) == 0 and n_chip & (n_chip - 1) == 0
    assert n_chip % min(n_chip, 4) == 0 and steps == 2
    half, quarter = length // 2, length // 4
    assert size == quarter and VALID % quarter == 0
    t = tables(length, size, VALID)
    rows = t["first"].shape[0] // 2
    names = ("first", "cos", "sin", "small", "base", "back", "last")
    count = tile_count * min(n_chip, 4) * steps
    levels = (n_tile - 1).bit_length()
    blocks = VALID // quarter
    shape = jax.ShapeDtypeStruct
    vmem, dma = pltpu.VMEM, pltpu.SemaphoreType.DMA
    operands = orient_ids, tile_offsets, micrograph_tiles, library, *[t[name] for name in names]
    both = pl.pallas_call(
        functools.partial(search_kernel, n_tile, n_orient, VALID),
        out_shape=shape((2, 2, VALID, VALID), bf16),
        in_specs=[HBM] * 11,
        out_specs=VMEM,
        scratch_shapes=[
            pltpu.SMEM(orient_ids.shape, jnp.int32),
            pltpu.SMEM(tile_offsets.shape, jnp.int32),
            vmem(micrograph_tiles.shape, bf16),
            vmem(library.shape, bf16),
            *[vmem(t[name].shape, bf16) for name in names],
            *[vmem((tile_count, rows, length), f32)] * 2,
            vmem((tile_count, 2 * rows, length), bf16),
            *[vmem((levels, rows, half), bf16)] * 2,
            vmem((2, rows, half), f32),
            vmem((steps, size, size), bf16),
            vmem((steps, n_tile - 1, size, size), bf16),
            vmem((n_chip, steps, size, size), bf16),
            *[vmem((tile_count, rows, length), bf16)] * 3,
            vmem((rows, length), bf16),
            vmem((count, rows, 2 * length), bf16),
            vmem((count, rows, length), bf16),
            vmem((count, 8, quarter), f32),
            vmem((blocks, length, count * quarter), bf16),
            vmem((2, blocks, 3, VALID, quarter), f32),
            *[vmem((blocks, 3, VALID, quarter), bf16)] * 2,
            dma((11,)),
            *[dma((steps, n_tile - 1))] * 2,
            *[dma((steps, n_chip - 1))] * 2,
            *[dma((blocks,))] * 2,
            *[dma((levels, 2))] * 2,
            *[dma((2,))] * 2,
            *[dma((blocks, 2))] * 2,
        ],
        compiler_params=pltpu.CompilerParams(
            collective_id=0, has_side_effects=True, vmem_limit_bytes=GRANT
        ),
    )(*[pltpu.with_memory_space_constraint(jnp.asarray(v), pltpu.HBM) for v in operands])
    return (both[0].astype(f32), both[1].astype(f32))


def solution(mesh):
    placed = (
        P("tile", None, None),
        P("tile", None),
        P("tile", "orient", None, None),
        P("orient", None),
    )
    return jax.shard_map(
        functools.partial(body, mesh.shape["tile"], mesh.shape["orient"]),
        mesh=mesh,
        in_specs=placed,
        out_specs=(P("tile", None, None), P("tile", None, None)),
        check_vma=False,
    )
```
